512 devices in a mesh: rep: 32 (over z, x), shard: 16 (over y, core).
Axes of the slice: x: 4, y: 8, z: 8, core: 2. Of those that a mesh axis runs over, the one named last changes fastest.
Arguments:
- grads: float32 [32, 32, 32, 5120], P('rep', 'shard'), may hold values from -1000 to 1000
- weight: float32 [32, 32, 5120], P('shard'), may hold values from -6 to 6
- moment_one: float32 [32, 32, 5120], P('shard', 'rep'), may hold values from -6 to 6
- moment_two: float32 [32, 32, 5120], P('shard', 'rep'), may hold values from 0.1 to 3
Outputs:
- new_weight: float32 [32, 32, 5120], P('shard')
- new_moment_one: float32 [32, 32, 5120], P('shard', 'rep')
- new_moment_two: float32 [32, 32, 5120], P('shard', 'rep')
The draws below stay inside these ranges and needn't reach their ends.
All inputs are finite; a program needn't handle non-finite values.
Results may differ from the reference program's by a relative error of at most 0.0003.
Values sent between devices are 32-bit elements; how exact they have to be, the bound alone decides.
A program may use at most 64 MiB of HBM per device.

```python
import math
import jax
import jax.numpy as jnp
from jax import lax

COLS = 5120
STEP = 100
REPLICAS = 32
TRIM = 4
SROWS = 32
RROWS = 32
PARAMS = 5242880


def draw_grads(key, part):
    keys = jax.random.split(key, 7)
    first = jnp.arange(SROWS, dtype=jnp.float32) / max(SROWS - 1, 1)
    second = jnp.arange(RROWS, dtype=jnp.float32) / max(RROWS - 1, 1)
    rough = jax.random.uniform(keys[0], (SROWS, RROWS), jnp.float32, 0.7, 1.4)
    row_scale = (3.0 ** first)[:, None] * (3.3 ** second)[None, :] * rough
    col_scale = jnp.exp(jax.random.uniform(keys[1], (COLS,), jnp.float32, -0.693, 0.693))
    scale = row_scale[:, :, None] * col_scale[None, None, :]
    common = jnp.clip(jax.random.normal(keys[2], (SROWS, RROWS, COLS), jnp.float32), -5.0, 5.0) * scale
    noise = 1.5 * jnp.clip(jax.random.normal(keys[3], (REPLICAS, SROWS, RROWS, COLS), jnp.float32), -5.0, 5.0)
    flips = jax.random.uniform(keys[4], (REPLICAS, SROWS, RROWS, COLS), jnp.float32) < 0.0625
    signs = jnp.where(jax.random.uniform(keys[5], (REPLICAS, SROWS, RROWS, COLS), jnp.float32) < 0.5, -20.0, 20.0)
    outlier = jnp.where(flips, signs, 0.0)
    values = common[None] + (noise + outlier) * scale[None]
    shape = (REPLICAS, SROWS, RROWS, COLS)
    replica_index = lax.broadcasted_iota(jnp.int32, shape, 0)
    copy_mark = jax.random.randint(keys[6], shape, 0, 4) == 0
    own_value = jnp.logical_not(copy_mark) | (replica_index == 0)
    source = lax.cummax(jnp.where(own_value, replica_index, jnp.zeros_like(replica_index)), axis=0)
    return jnp.take_along_axis(values, source, axis=0)


def block_scale(own_key, extent, pieces, smallest, largest):
    factor_of, own = 1.0, jax.random.fold_in(own_key, 6)
    for position, shards_of in pieces:
        draws = jnp.exp(jax.random.uniform(jax.random.fold_in(own, position), (shards_of,), jnp.float32, smallest / len(pieces), largest / len(pieces)))
        factor_of = factor_of * jnp.repeat(draws, extent[position] // shards_of).reshape([-1 if axis == position else 1 for axis in range(len(extent))])
    return factor_of


def centred(key, extent, spread, bound, pieces=(), kind=jnp.bfloat16):
    gain = block_scale(key, extent, pieces, -0.22, 0.18) if pieces else 1.0
    drawn = jax.random.normal(key, extent, jnp.float32) * spread * gain
    return jnp.minimum(jnp.maximum(drawn, -bound), bound).astype(kind)


def setup_inputs(seed: int = 0) -> dict:
    key_list = jax.random.split(jax.random.key(seed), 5)
    grads = draw_grads(jax.random.fold_in(key_list[4], 71), 0)
    weight = centred(key_list[1], (SROWS, RROWS, COLS), 1.0, 6.0, ((0, 16),), jnp.float32)
    moment_one = centred(key_list[2], (SROWS, RROWS, COLS), 1.0, 6.0, ((0, 16), (1, 32)), jnp.float32)
    moment_two = jnp.clip(jnp.exp(math.log(3.0) - 3.4011974 * jax.random.uniform(key_list[3], (SROWS, RROWS, COLS), jnp.float32) ** block_scale(key_list[3], (SROWS, RROWS, COLS), ((0, 16), (1, 32)), -0.2, 0.2)), 0.1, 3.0)
    return {"grads": grads, "weight": weight, "moment_one": moment_one, "moment_two": moment_two}


def trimmed_block(block, trim_count):
    count = block.shape[0]
    order = jnp.arange(count, dtype=jnp.int32)
    lower = block[None, :, :] < block[:, None, :]
    equal = (block[None, :, :] == block[:, None, :]) & (order[None, :, None] < order[:, None, None])
    rank = lax.optimization_barrier(jnp.sum((lower | equal).astype(jnp.int32), axis=1))
    keep = (rank >= trim_count) & (rank < count - trim_count)
    kept = lax.optimization_barrier(jnp.sum(jnp.where(keep, block, jnp.zeros_like(block)), axis=0))
    return kept / (count - 2 * trim_count)

def trimmed_mean(values, trim_count):
    count, total = values.shape
    width = 512 if total % 512 == 0 else total
    blocks = values.reshape(count, total // width, width).transpose(1, 0, 2)
    result = lax.map(lambda item: trimmed_block(item, trim_count), blocks)
    return result.reshape(total)

def reference(grads, weight, moment_one, moment_two):
    flat = grads.reshape(grads.shape[0], -1)
    trimmed = trimmed_mean(flat, TRIM).reshape(weight.shape)
    total = jnp.sum(trimmed * trimmed)
    factor = jnp.minimum(1.0, 1.0 / jnp.sqrt(total / PARAMS + 1e-12))
    clipped = factor * trimmed
    new_one = 0.9 * moment_one + 0.1 * clipped
    new_two = 0.95 * moment_two + 0.05 * clipped * clipped
    update = new_one / (1.0 - 0.9 ** STEP) / (jnp.sqrt(new_two / (1.0 - 0.95 ** STEP)) + 1e-08)
    new_weight = weight - 0.05 * (update + 0.1 * weight)
    return (new_weight, new_one, new_two)
```

```python
import jax
import jax.numpy as jnp
from jax import lax
from jax.experimental import pallas as pl
from jax.experimental.pallas import tpu as pltpu
from jax.sharding import PartitionSpec as P

STEP = 100
MESH = pl.DeviceIdType.MESH
NZ, NX = 8, 4
REPS, SHARDS = 32, 16
TRIM = 4
F32 = jnp.float32

SORT8 = (
    (0, 1), (2, 3), (4, 5), (6, 7),
    (0, 2), (1, 3), (4, 6), (5, 7),
    (1, 2), (5, 6),
    (0, 4), (1, 5), (2, 6), (3, 7),
    (2, 4), (3, 5),
    (1, 2), (3, 4), (5, 6),
)


def exchange(values, i, j):
    a, b = values[i], values[j]
    values[i], values[j] = jnp.minimum(a, b), jnp.maximum(a, b)


def sort8(values):
    values = list(values)
    for i, j in SORT8:
        exchange(values, i, j)
    return values[:4], values[4:]


def add_all(values):
    values = list(values)
    while len(values) > 1:
        values = [a + b for a, b in zip(values[::2], values[1::2])] + (
            [values[-1]] if len(values) % 2 else []
        )
    return values[0]


def merge(one, two):
    (low_a, high_a), (low_b, high_b) = one, two
    low = [jnp.minimum(low_a[i], low_b[3 - i]) for i in range(4)]
    high = [jnp.maximum(high_a[i], high_b[3 - i]) for i in range(4)]
    for i, j in ((0, 2), (1, 3), (0, 1), (2, 3)):
        exchange(low, i, j)
        exchange(high, i, j)
    return (low, high), middle(one, two)


def middle(one, two):
    (low_a, high_a), (low_b, high_b) = one, two
    return add_all(
        [jnp.maximum(low_a[i], low_b[3 - i]) for i in range(4)]
        + [jnp.minimum(high_a[i], high_b[3 - i]) for i in range(4)]
    )


def kept_sum(values):
    groups = [sort8(values[8 * g : 8 * g + 8]) for g in range(4)]
    left, left_sum = merge(groups[0], groups[1])
    right, right_sum = merge(groups[2], groups[3])
    return left_sum + right_sum + middle(left, right)


def row_of(ref, r):
    return ref.at[:, r // 8, :, lax.rem(r, 8), :]


def tiles(block):
    return block.reshape(2, 4, 8, 40, 128).transpose(0, 1, 3, 2, 4)


def kernel(
    params,
    grads,
    weight,
    one_ref,
    two_ref,
    new_weight,
    new_one_ref,
    new_two_ref,
    received,
    row,
    outgoing,
    trimmed,
    partial,
    sums,
    local_sem,
    send_sem,
    recv_sem,
    sum_send,
    sum_recv,
    gather_send,
    z_recv,
    x_recv,
    half_recv,
    out_sem,
):
    me = lax.axis_index("rep")
    shard = lax.axis_index("shard")
    z, x = me // NX, lax.rem(me, NX)

    def at(dz, dx):
        return lax.rem(z + dz, NZ) * NX + lax.rem(x + dx, NX)

    own_row = pltpu.make_async_copy(row_of(weight, me), row, local_sem.at[0])
    own_row.start()
    own_grads = pltpu.make_async_copy(
        row_of(grads, me), received.at[me], local_sem.at[1]
    )
    own_grads.start()

    barrier = pltpu.get_barrier_semaphore()
    for i in range(1, REPS):
        pl.semaphore_signal(
            barrier, inc=1, device_id=(lax.rem(me + i, REPS), shard), device_id_type=MESH
        )
    for i in range(1, SHARDS):
        pl.semaphore_signal(
            barrier, inc=1, device_id=(me, lax.rem(shard + i, SHARDS)), device_id_type=MESH
        )
    pl.semaphore_wait(barrier, REPS + SHARDS - 2)

    for dz in (4, 3, 5, 2, 6, 1, 7, 0):
        for dx in (2, 1, 3, 0):
            if dz or dx:
                peer = at(dz, dx)
                pltpu.make_async_remote_copy(
                    src_ref=row_of(grads, peer),
                    dst_ref=received.at[me],
                    send_sem=send_sem,
                    recv_sem=recv_sem,
                    device_id=(peer, shard),
                    device_id_type=MESH,
                ).start()
    own_row.wait()
    own_grads.wait()
    others = received.at[pl.ds(0, REPS - 1)]
    pltpu.make_async_copy(others, others, recv_sem).wait()

    def block(j, squares):
        h, rows = j // 5, pl.ds(pl.multiple_of(lax.rem(j, 5) * 8, 8), 8)
        mean = kept_sum([received[i, h, rows, :] for i in range(REPS)]) / (REPS - 2 * TRIM)
        trimmed[h, rows, :] = mean
        return squares + mean * mean

    squares = lax.fori_loop(0, 10, block, jnp.zeros((8, 128), F32))
    total = jnp.sum(squares, axis=0, keepdims=True)

    for stage, (count, mine, device) in enumerate(
        (
            (REPS, me, lambda p: (p, shard)),
            (SHARDS, shard, lambda p: (me, p)),
        )
    ):
        partial[stage] = total
        sums[stage, pl.ds(mine, 1), :] = total
        for i in range(1, count):
            pltpu.make_async_remote_copy(
                src_ref=partial.at[stage],
                dst_ref=sums.at[stage, pl.ds(mine, 1), :],
                send_sem=sum_send.at[stage],
                recv_sem=sum_recv.at[stage],
                device_id=device(lax.rem(mine + i, count)),
                device_id_type=MESH,
            ).start()
        got = sums.at[stage, pl.ds(0, count - 1), :]
        pltpu.make_async_copy(got, got, sum_recv.at[stage]).wait()
        total = jnp.sum(sums[stage, 0:count, :], axis=0, keepdims=True)
    total = jnp.sum(total, axis=1, keepdims=True)
    factor = jnp.minimum(1.0, 1.0 / jnp.sqrt(total / params + 1e-12))

    clipped = factor * trimmed[...]
    new_one = 0.9 * one_ref[...] + 0.1 * clipped
    new_two = 0.95 * two_ref[...] + 0.05 * clipped * clipped
    update = new_one / (1.0 - 0.9**STEP) / (jnp.sqrt(new_two / (1.0 - 0.95**STEP)) + 1e-08)
    owned = row[...]
    outgoing[...] = owned - 0.05 * (update + 0.1 * owned)
    new_one_ref[...] = new_one
    new_two_ref[...] = new_two

    def at_row(r):
        return row_of(new_weight, r)

    def push(src, r, peer, sem):
        pltpu.make_async_remote_copy(
            src_ref=src,
            dst_ref=at_row(r),
            send_sem=gather_send,
            recv_sem=sem,
            device_id=(peer, shard),
            device_id_type=MESH,
        ).start()

    for dz in (1, 7, 2, 6, 3, 5, 4):
        push(outgoing, me, at(dz, 0), z_recv.at[z])
    for side, dx in enumerate((1, 3)):
        push(outgoing, me, at(0, dx), x_recv.at[side, z])
    keep = pltpu.make_async_copy(outgoing, at_row(me), out_sem)
    keep.start()

    def from_x(dz):
        zz = lax.rem(z + dz, NZ)
        for side, dx in enumerate((1, 3)):
            r = at(dz, NX - dx)
            view = at_row(r)
            pltpu.make_async_copy(view, view, x_recv.at[side, zz]).wait()
            half = new_weight.at[side, r // 8, :, lax.rem(r, 8), :]
            pltpu.make_async_remote_copy(
                src_ref=half,
                dst_ref=half,
                send_sem=gather_send,
                recv_sem=half_recv,
                device_id=(at(0, dx), shard),
                device_id_type=MESH,
            ).start()

    order = (0, 1, 7, 2, 6, 3, 5, 4)
    for k, dz in enumerate(order[1:]):
        zz = lax.rem(z + dz, NZ)
        r = at(dz, 0)
        view = at_row(r)
        pltpu.make_async_copy(view, view, z_recv.at[zz]).wait()
        for side, dx in enumerate((1, 3)):
            push(view, r, at(0, dx), x_recv.at[side, zz])
        from_x(order[k])
    from_x(order[-1])
    eight = received.at[pl.ds(0, 8)]
    pltpu.make_async_copy(eight, eight, half_recv).wait()
    keep.wait()

    pltpu.make_async_copy(others, others, send_sem).wait()
    pltpu.make_async_copy(others, others, gather_send).wait()
    for stage, count in enumerate((REPS, SHARDS)):
        got = sums.at[stage, pl.ds(0, count - 1), :]
        pltpu.make_async_copy(got, got, sum_send.at[stage]).wait()


def on_device(grads, weight, moment_one, moment_two):
    params = weight.shape[0] * SHARDS * weight.shape[1] * weight.shape[2]
    vmem = pl.BlockSpec(memory_space=pltpu.VMEM)
    hbm = pl.BlockSpec(memory_space=pltpu.HBM)
    unit = (2, 40, 128)
    dma = pltpu.SemaphoreType.DMA
    new_weight, new_one, new_two = pl.pallas_call(
        lambda *refs: kernel(params, *refs),
        name="robust_step",
        out_shape=(
            jax.ShapeDtypeStruct((2, 4, 40, 8, 128), F32),
            jax.ShapeDtypeStruct(unit, F32),
            jax.ShapeDtypeStruct(unit, F32),
        ),
        in_specs=[hbm, hbm, vmem, vmem],
        out_specs=(vmem, vmem, vmem),
        scratch_shapes=[
            pltpu.VMEM((REPS,) + unit, F32),
            pltpu.VMEM(unit, F32),
            pltpu.VMEM(unit, F32),
            pltpu.VMEM(unit, F32),
            pltpu.VMEM((2, 1, 128), F32),
            pltpu.VMEM((2, REPS, 128), F32),
            dma((2,)),
            dma,
            dma,
            dma((2,)),
            dma((2,)),
            dma,
            dma((NZ,)),
            dma((2, NZ)),
            dma,
            dma,
        ],
        compiler_params=pltpu.CompilerParams(
            collective_id=0, has_side_effects=True
        ),
    )(tiles(grads[0]), tiles(weight), moment_one.reshape(unit), moment_two.reshape(unit))
    return (
        new_weight.transpose(0, 1, 3, 2, 4).reshape(weight.shape),
        new_one.reshape(moment_one.shape),
        new_two.reshape(moment_two.shape),
    )


def solution(mesh):
    return jax.shard_map(
        on_device,
        mesh=mesh,
        in_specs=(
            P("rep", "shard", None, None),
            P("shard", None, None),
            P("shard", "rep", None),
            P("shard", "rep", None),
        ),
        out_specs=(P("shard", None, None), P("shard", "rep", None), P("shard", "rep", None)),
        check_vma=False,
    )
```

```python
import jax
import jax.numpy as jnp
from jax import lax
from jax.experimental import pallas as pl
from jax.experimental.pallas import tpu as pltpu
from jax.sharding import PartitionSpec as P

STEP = 100
MESH = pl.DeviceIdType.MESH
NZ, NX, NY = 8, 4, 8
REPS, SHARDS = 32, 16
TRIM = 4
SPLIT = 24
F32 = jnp.float32

SORT8 = (
    (0, 1), (2, 3), (4, 5), (6, 7),
    (0, 2), (1, 3), (4, 6), (5, 7),
    (1, 2), (5, 6),
    (0, 4), (1, 5), (2, 6), (3, 7),
    (2, 4), (3, 5),
    (1, 2), (3, 4), (5, 6),
)


def exchange(values, i, j):
    a, b = values[i], values[j]
    values[i], values[j] = jnp.minimum(a, b), jnp.maximum(a, b)


def sort8(values):
    values = list(values)
    for i, j in SORT8:
        exchange(values, i, j)
    return values[:4], values[4:]


def add_all(values):
    values = list(values)
    while len(values) > 1:
        values = [a + b for a, b in zip(values[::2], values[1::2])] + (
            [values[-1]] if len(values) % 2 else []
        )
    return values[0]


def merge(one, two):
    (low_a, high_a), (low_b, high_b) = one, two
    low = [jnp.minimum(low_a[i], low_b[3 - i]) for i in range(4)]
    high = [jnp.maximum(high_a[i], high_b[3 - i]) for i in range(4)]
    for i, j in ((0, 2), (1, 3), (0, 1), (2, 3)):
        exchange(low, i, j)
        exchange(high, i, j)
    return (low, high), middle(one, two)


def middle(one, two):
    (low_a, high_a), (low_b, high_b) = one, two
    return add_all(
        [jnp.maximum(low_a[i], low_b[3 - i]) for i in range(4)]
        + [jnp.minimum(high_a[i], high_b[3 - i]) for i in range(4)]
    )


def kept_sum(values):
    groups = [sort8(values[8 * g : 8 * g + 8]) for g in range(4)]
    left, left_sum = merge(groups[0], groups[1])
    right, right_sum = merge(groups[2], groups[3])
    return left_sum + right_sum + middle(left, right)


def row_of(ref, r):
    return ref.at[:, r // 8, :, lax.rem(r, 8), :]


def tiles(block):
    return block.reshape(2, 4, 8, 40, 128).transpose(0, 1, 3, 2, 4)


def kernel(
    params,
    grads,
    weight,
    moment_one,
    moment_two,
    new_weight,
    new_one_ref,
    new_two_ref,
    received,
    row,
    one_ref,
    two_ref,
    outgoing,
    trimmed,
    partial,
    sums,
    local_sem,
    send_sem,
    recv_sem,
    sum_send,
    sum_recv,
    gather_send,
    z_recv,
    x_recv,
    half_recv,
    last_recv,
    four_recv,
    out_sem,
    above_sem,
    ring_sem,
    core_sem,
):
    me = lax.axis_index("rep")
    shard = lax.axis_index("shard")
    z, x = me // NX, lax.rem(me, NX)

    def at(dz, dx):
        return lax.rem(z + dz, NZ) * NX + lax.rem(x + dx, NX)

    y, core = shard // 2, lax.rem(shard, 2)

    def in_y(dy):
        return lax.rem(y + dy, NY) * 2 + core

    local = [
        pltpu.make_async_copy(src, dst, local_sem.at[i])
        for i, (src, dst) in enumerate(
            (
                (row_of(grads, me), received.at[me]),
                (row_of(weight, me), row),
                (moment_one, one_ref),
                (moment_two, two_ref),
            )
        )
    ]
    for copy in local:
        copy.start()

    barrier = pltpu.get_barrier_semaphore()

    def signal(sem, rep, sh):
        pl.semaphore_signal(sem, inc=1, device_id=(rep, sh), device_id_type=MESH)

    for dx in (2, 1, 3):
        signal(barrier, at(0, dx), shard)
    for dy in (1, NY - 1):
        signal(barrier, me, in_y(dy))

    @pl.when(core == 0)
    def _():
        signal(barrier, me, shard + 1)

    pl.semaphore_wait(barrier, 5 + (z > 0).astype(jnp.int32) + core)

    @pl.when(z < NZ - 1)
    def _():
        signal(barrier, me + NX, shard)

    @pl.loop(0, z)
    def _(zz):
        signal(above_sem.at[z], zz * NX + x, shard)

    def send_grads(zz, dx):
        peer = zz * NX + lax.rem(x + dx, NX)
        pltpu.make_async_remote_copy(
            src_ref=row_of(grads, peer),
            dst_ref=received.at[me],
            send_sem=send_sem,
            recv_sem=recv_sem,
            device_id=(peer, shard),
            device_id_type=MESH,
        ).start()

    @pl.loop(0, z)
    def _(zz):
        for dx in (2, 1, 3, 0):
            send_grads(zz, dx)

    for dx in (2, 1, 3):
        send_grads(z, dx)

    @pl.loop(z + 1, NZ)
    def _(zz):
        pl.semaphore_wait(above_sem.at[zz], 1)
        for dx in (2, 1, 3, 0):
            send_grads(zz, dx)

    @pl.when(core == 0)
    def _():
        pl.semaphore_wait(core_sem, 1)

    signal(core_sem, me, shard + 1 - 2 * core)

    @pl.when(core == 1)
    def _():
        pl.semaphore_wait(core_sem, 1)

    for r in range(NY // 2 - 1):
        for side, dy in enumerate((1, NY - 1)):
            signal(ring_sem.at[r, side], me, in_y(dy))
        for side in range(2):
            pl.semaphore_wait(ring_sem.at[r, side], 1)

    for copy in local:
        copy.wait()
    others = received.at[pl.ds(0, REPS - 1)]
    pltpu.make_async_copy(others, others, recv_sem).wait()

    def block(j, squares):
        h, rows = j // 5, pl.ds(pl.multiple_of(lax.rem(j, 5) * 8, 8), 8)
        mean = kept_sum([received[i, h, rows, :] for i in range(REPS)]) / (REPS - 2 * TRIM)
        trimmed[h, rows, :] = mean
        return squares + mean * mean

    squares = lax.fori_loop(0, 10, block, jnp.zeros((8, 128), F32))
    total = jnp.sum(squares, axis=0, keepdims=True)

    stages = (
        (2 * REPS, me * 2 + core, lambda p: (p // 2, y * 2 + lax.rem(p, 2))),
        (NY, y, lambda p: (me, p * 2 + core)),
    )
    for stage, (count, mine, device) in enumerate(stages):
        partial[stage] = total
        sums[stage, pl.ds(mine, 1), :] = total
        for i in range(1, count):
            pltpu.make_async_remote_copy(
                src_ref=partial.at[stage],
                dst_ref=sums.at[stage, pl.ds(mine, 1), :],
                send_sem=sum_send.at[stage],
                recv_sem=sum_recv.at[stage],
                device_id=device(lax.rem(mine + i, count)),
                device_id_type=MESH,
            ).start()
        got = sums.at[stage, pl.ds(0, count - 1), :]
        pltpu.make_async_copy(got, got, sum_recv.at[stage]).wait()
        total = jnp.sum(sums[stage, 0:count, :], axis=0, keepdims=True)
    total = jnp.sum(total, axis=1, keepdims=True)
    factor = jnp.minimum(1.0, 1.0 / jnp.sqrt(total / params + 1e-12))

    clipped = factor * trimmed[...]
    new_one = 0.9 * one_ref[...] + 0.1 * clipped
    new_two = 0.95 * two_ref[...] + 0.05 * clipped * clipped
    update = new_one / (1.0 - 0.9**STEP) / (jnp.sqrt(new_two / (1.0 - 0.95**STEP)) + 1e-08)
    owned = row[...]
    outgoing[...] = owned - 0.05 * (update + 0.1 * owned)
    new_one_ref[...] = new_one
    new_two_ref[...] = new_two

    first, last = pl.ds(0, SPLIT), pl.ds(SPLIT, 40 - SPLIT)
    right_left = (1, NX - 1)

    def part(r, tiles):
        return new_weight.at[:, r // 8, tiles, lax.rem(r, 8), :]

    def half(r, h):
        return new_weight.at[h, r // 8, first, lax.rem(r, 8), :]

    def four(zz):
        return new_weight.at[:, zz // 2, last, pl.ds(lax.rem(zz, 2) * 4, 4), :]

    def half_four(zz, h):
        return new_weight.at[h, zz // 2, last, pl.ds(lax.rem(zz, 2) * 4, 4), :]

    def push(src, dst, peer, sem):
        pltpu.make_async_remote_copy(
            src_ref=src,
            dst_ref=dst,
            send_sem=gather_send,
            recv_sem=sem,
            device_id=(peer, shard),
            device_id_type=MESH,
        ).start()

    def came(view, sem):
        pltpu.make_async_copy(view, view, sem).wait()

    def zs(dz):
        return lax.rem(z + dz, NZ)

    def along_x(dz, src=None):
        view = part(at(dz, 0), first)
        for side, dx in enumerate(right_left):
            push(view if src is None else src, view, at(0, dx), x_recv.at[side, zs(dz)])

    def relay_x(dz):
        for side, dx in enumerate(right_left):
            r = at(dz, NX - dx)
            came(part(r, first), x_recv.at[side, zs(dz)])
            push(half(r, side), half(r, side), at(0, dx), half_recv)

    def from_z(dz):
        came(part(at(dz, 0), first), z_recv.at[zs(dz)])

    own_first, own_last = outgoing.at[:, first, :], outgoing.at[:, last, :]
    for dz in (2, 6, 1, 7):
        push(own_first, part(me, first), at(dz, 0), z_recv.at[z])
    along_x(0, own_first)
    for dx in (2, 1, 3):
        push(own_last, part(me, last), at(0, dx), last_recv)
    keep = pltpu.make_async_copy(outgoing, row_of(new_weight, me), out_sem)
    keep.start()

    for dz in (1, 7):
        from_z(dz)
        along_x(dz)
    for dz, on in ((6, 1), (2, 7)):
        from_z(dz)
        r, h = at(dz, 0), (0 if on == 1 else 1)
        push(part(r, first), part(r, first), at(on, 0), z_recv.at[zs(dz)])
        push(half(r, h), half(r, h), at(2 * on % NZ, 0), z_recv.at[zs(dz)])
        along_x(dz)
    relay_x(0)
    three = received.at[pl.ds(0, 3), :, last, :]
    came(three, last_recv)
    keep.wait()
    for dz in (2, 6, 1, 7):
        push(four(z), four(z), at(dz, 0), four_recv.at[z])
    for dz in (1, 7, 2, 6):
        relay_x(dz)
    for dz in (3, 5, 4):
        from_z(dz)
        along_x(dz)
    for dz, on in ((6, 1), (2, 7)):
        zz, h = zs(dz), (0 if on == 1 else 1)
        came(four(zz), four_recv.at[zz])
        push(four(zz), four(zz), at(on, 0), four_recv.at[zz])
        push(half_four(zz, h), half_four(zz, h), at(2 * on % NZ, 0), four_recv.at[zz])
    for dz in (3, 5, 4):
        relay_x(dz)
    for dz in (1, 7, 3, 5, 4):
        came(four(zs(dz)), four_recv.at[zs(dz)])
    came(received.at[pl.ds(0, 8), :, first, :], half_recv)

    pltpu.make_async_copy(others, others, send_sem).wait()
    pltpu.make_async_copy(others, others, gather_send).wait()
    for stage, (count, _, _) in enumerate(stages):
        got = sums.at[stage, pl.ds(0, count - 1), :]
        pltpu.make_async_copy(got, got, sum_send.at[stage]).wait()


def store(*refs):
    *pairs, sems = refs
    copies = [pltpu.make_async_copy(pairs[i], pairs[i + 3], sems.at[i]) for i in range(3)]
    for copy in copies:
        copy.start()
    for copy in copies:
        copy.wait()


def pinned(array):
    return pltpu.with_memory_space_constraint(array, pltpu.HBM)


def on_device(grads, weight, moment_one, moment_two):
    params = weight.shape[0] * SHARDS * weight.shape[1] * weight.shape[2]
    vmem = pl.BlockSpec(memory_space=pltpu.VMEM)
    hbm = pl.BlockSpec(memory_space=pltpu.HBM)
    unit = (2, 40, 128)
    dma, regular = pltpu.SemaphoreType.DMA, pltpu.SemaphoreType.REGULAR
    results = pl.pallas_call(
        lambda *refs: kernel(params, *refs),
        name="robust_step",
        out_shape=(
            pltpu.VMEM((2, 4, 40, 8, 128), F32),
            pltpu.VMEM(unit, F32),
            pltpu.VMEM(unit, F32),
        ),
        in_specs=[hbm] * 4,
        out_specs=(vmem, vmem, vmem),
        scratch_shapes=[
            pltpu.VMEM((REPS,) + unit, F32),
            pltpu.VMEM(unit, F32),
            pltpu.VMEM(unit, F32),
            pltpu.VMEM(unit, F32),
            pltpu.VMEM(unit, F32),
            pltpu.VMEM(unit, F32),
            pltpu.VMEM((2, 1, 128), F32),
            pltpu.VMEM((2, 2 * REPS, 128), F32),
            dma((4,)),
            dma,
            dma,
            dma((2,)),
            dma((2,)),
            dma,
            dma((NZ,)),
            dma((2, NZ)),
            dma,
            dma,
            dma((NZ,)),
            dma,
            regular((NZ,)),
            regular((NY // 2 - 1, 2)),
            regular,
        ],
        compiler_params=pltpu.CompilerParams(
            collective_id=0, has_side_effects=True, vmem_limit_bytes=32 << 20
        ),
    )(pinned(tiles(grads[0])), pinned(tiles(weight)), pinned(moment_one.reshape(unit)), pinned(moment_two.reshape(unit)))
    new_weight, new_one, new_two = pl.pallas_call(
        store,
        name="store",
        out_shape=tuple(jax.ShapeDtypeStruct(r.shape, F32) for r in results),
        in_specs=[vmem] * 3,
        out_specs=(hbm,) * 3,
        scratch_shapes=[dma((3,))],
        compiler_params=pltpu.CompilerParams(vmem_limit_bytes=16 << 20),
    )(*results)
    return (
        new_weight.transpose(0, 1, 3, 2, 4).reshape(weight.shape),
        new_one.reshape(moment_one.shape),
        new_two.reshape(moment_two.shape),
    )


def solution(mesh):
    return jax.shard_map(
        on_device,
        mesh=mesh,
        in_specs=(
            P("rep", "shard", None, None),
            P("shard", None, None),
            P("shard", "rep", None),
            P("shard", "rep", None),
        ),
        out_specs=(P("shard", None, None), P("shard", "rep", None), P("shard", "rep", None)),
        check_vma=False,
    )
```

```python
import jax
import jax.numpy as jnp
from jax import lax
from jax.experimental import pallas as pl
from jax.experimental.pallas import tpu as pltpu
from jax.sharding import PartitionSpec as P

STEP = 100
MESH = pl.DeviceIdType.MESH
NZ, NX, NY = 8, 4, 8
REPS, SHARDS = 32, 16
TRIM = 4
SPLIT = 24
F32 = jnp.float32

SORT8 = (
    (0, 1), (2, 3), (4, 5), (6, 7),
    (0, 2), (1, 3), (4, 6), (5, 7),
    (1, 2), (5, 6),
    (0, 4), (1, 5), (2, 6), (3, 7),
    (2, 4), (3, 5),
    (1, 2), (3, 4), (5, 6),
)


def exchange(values, i, j):
    a, b = values[i], values[j]
    values[i], values[j] = jnp.minimum(a, b), jnp.maximum(a, b)


def sort8(values):
    values = list(values)
    for i, j in SORT8:
        exchange(values, i, j)
    return values[:4], values[4:]


def add_all(values):
    values = list(values)
    while len(values) > 1:
        values = [a + b for a, b in zip(values[::2], values[1::2])] + (
            [values[-1]] if len(values) % 2 else []
        )
    return values[0]


def merge(one, two):
    (low_a, high_a), (low_b, high_b) = one, two
    low = [jnp.minimum(low_a[i], low_b[3 - i]) for i in range(4)]
    high = [jnp.maximum(high_a[i], high_b[3 - i]) for i in range(4)]
    for i, j in ((0, 2), (1, 3), (0, 1), (2, 3)):
        exchange(low, i, j)
        exchange(high, i, j)
    return (low, high), middle(one, two)


def middle(one, two):
    (low_a, high_a), (low_b, high_b) = one, two
    return add_all(
        [jnp.maximum(low_a[i], low_b[3 - i]) for i in range(4)]
        + [jnp.minimum(high_a[i], high_b[3 - i]) for i in range(4)]
    )


def row_of(ref, r):
    return ref.at[:, r // 8, :, lax.rem(r, 8), :]


def half_row(ref, r, h):
    return ref.at[h, r // 8, :, lax.rem(r, 8), :]


def bundle(h, slot):
    return h * 16 + slot


def direct(h, slot):
    return REPS + h * 16 + slot


def tiles(block):
    return block.reshape(2, 4, 8, 40, 128).transpose(0, 1, 3, 2, 4)


def kernel(
    params,
    grads,
    weight,
    moment_one,
    moment_two,
    new_weight,
    new_one_ref,
    new_two_ref,
    received,
    summary,
    row,
    one_ref,
    two_ref,
    outgoing,
    trimmed,
    partial,
    sums,
    local_sem,
    send_sem,
    bundle_recv,
    recv_sem,
    summary_send,
    summary_recv,
    sum_send,
    sum_recv,
    gather_send,
    z_recv,
    x_recv,
    half_recv,
    last_recv,
    four_recv,
    out_sem,
    above_sem,
    ring_sem,
    core_sem,
):
    me = lax.axis_index("rep")
    shard = lax.axis_index("shard")
    z, x = me // NX, lax.rem(me, NX)

    def at(dz, dx):
        return lax.rem(z + dz, NZ) * NX + lax.rem(x + dx, NX)

    y, core = shard // 2, lax.rem(shard, 2)

    def in_y(dy):
        return lax.rem(y + dy, NY) * 2 + core

    local = [
        pltpu.make_async_copy(src, dst, local_sem.at[i])
        for i, (src, dst) in enumerate(
            (
                (half_row(grads, me, 0), received.at[direct(0, x)]),
                (half_row(grads, me, 1), received.at[direct(1, x)]),
                (half_row(grads, at(NZ - 1, 0), 0), received.at[bundle(0, x)]),
                (half_row(grads, at(1, 0), 1), received.at[bundle(1, x)]),
                (row_of(weight, me), row),
                (moment_one, one_ref),
                (moment_two, two_ref),
            )
        )
    ]
    for copy in local:
        copy.start()

    barrier = pltpu.get_barrier_semaphore()

    def signal(sem, rep, sh):
        pl.semaphore_signal(sem, inc=1, device_id=(rep, sh), device_id_type=MESH)

    for dx in (2, 1, 3):
        signal(barrier, at(0, dx), shard)
    for dy in (1, NY - 1):
        signal(barrier, me, in_y(dy))

    @pl.when(core == 0)
    def _():
        signal(barrier, me, shard + 1)

    pl.semaphore_wait(barrier, 5 + (z > 0).astype(jnp.int32) + core)

    @pl.when(z < NZ - 1)
    def _():
        signal(barrier, me + NX, shard)

    @pl.loop(0, z)
    def _(zz):
        signal(above_sem.at[z], zz * NX + x, shard)

    def send_half(row_index, h, slot, peer, sem):
        pltpu.make_async_remote_copy(
            src_ref=half_row(grads, row_index, h),
            dst_ref=received.at[slot],
            send_sem=send_sem,
            recv_sem=sem,
            device_id=(peer, shard),
            device_id_type=MESH,
        ).start()

    def towards(zz):
        d = lax.rem(zz - z + NZ, NZ)
        down = (d > NZ // 2).astype(jnp.int32)
        distance = d + down * (NZ - 2 * d)
        return down, distance, d != NZ // 2

    def send_bundles(zz):
        down, distance, far = towards(zz)
        beyond = lax.rem(zz + 1 + down * (NZ - 2), NZ)

        @pl.when(far)
        def _():
            for dx in (2, 1, 3, 0):
                xx = lax.rem(x + dx, NX)
                slot = bundle(1 - down, distance * NX + x)
                send_half(beyond * NX + xx, 1 - down, slot, zz * NX + xx, bundle_recv.at[1 - down])

    def send_direct(zz):
        down, distance, far = towards(zz)

        @pl.when(far)
        def _():
            for dx in (2, 1, 3, 0):
                xx = lax.rem(x + dx, NX)
                slot = direct(down, distance * NX + x)
                send_half(zz * NX + xx, down, slot, zz * NX + xx, recv_sem)

    pl.loop(0, z)(send_bundles)

    for dx in (2, 1, 3):
        send_half(at(NZ - 1, dx), 0, bundle(0, x), at(0, dx), bundle_recv.at[0])
        send_half(at(1, dx), 1, bundle(1, x), at(0, dx), bundle_recv.at[1])

    pl.loop(0, z)(send_direct)

    for dx in (2, 1, 3):
        for h in range(2):
            send_half(at(0, dx), h, direct(h, x), at(0, dx), recv_sem)

    @pl.loop(z + 1, NZ)
    def _(zz):
        pl.semaphore_wait(above_sem.at[zz], 1)
        send_bundles(zz)
        send_direct(zz)

    @pl.when(core == 0)
    def _():
        pl.semaphore_wait(core_sem, 1)

    signal(core_sem, me, shard + 1 - 2 * core)

    @pl.when(core == 1)
    def _():
        pl.semaphore_wait(core_sem, 1)

    for r in range(NY // 2 - 1):
        for side, dy in enumerate((1, NY - 1)):
            signal(ring_sem.at[r, side], me, in_y(dy))
        for side in range(2):
            pl.semaphore_wait(ring_sem.at[r, side], 1)

    for copy in local:
        copy.wait()
    def came(view, sem):
        pltpu.make_async_copy(view, view, sem).wait()

    def halves(n):
        return received.at[pl.ds(0, n)]

    def condense(first_slot):
        @pl.loop(0, 5)
        def _(j):
            rows = pl.ds(pl.multiple_of(j * 8, 8), 8)
            values = [received[first_slot + i, rows, :] for i in range(16)]
            (low, high), rest = merge(sort8(values[:8]), sort8(values[8:]))
            for i, value in enumerate(low + high + [rest]):
                received[first_slot + i, rows, :] = value

    for h, dz in enumerate((NZ - 1, 1)):
        came(halves(15), bundle_recv.at[h])
        condense(bundle(h, 0))
        pltpu.make_async_remote_copy(
            src_ref=received.at[pl.ds(bundle(h, 0), 9)],
            dst_ref=summary.at[h],
            send_sem=summary_send,
            recv_sem=summary_recv.at[h],
            device_id=(at(dz, 0), shard),
            device_id_type=MESH,
        ).start()
    came(halves(30), recv_sem)
    for h in range(2):
        condense(direct(h, 0))
    for h in range(2):
        came(halves(9), summary_recv.at[h])

    def block(j, squares):
        h, rows = j // 5, pl.ds(pl.multiple_of(lax.rem(j, 5) * 8, 8), 8)
        near = [received[direct(h, i), rows, :] for i in range(9)]
        far = [summary[h, i, rows, :] for i in range(9)]
        rest = middle((near[:4], near[4:8]), (far[:4], far[4:8]))
        mean = (near[8] + far[8] + rest) / (REPS - 2 * TRIM)
        trimmed[h, rows, :] = mean
        return squares + mean * mean

    squares = lax.fori_loop(0, 10, block, jnp.zeros((8, 128), F32))
    total = jnp.sum(squares, axis=0, keepdims=True)

    stages = (
        (2 * REPS, me * 2 + core, lambda p: (p // 2, y * 2 + lax.rem(p, 2))),
        (NY, y, lambda p: (me, p * 2 + core)),
    )
    for stage, (count, mine, device) in enumerate(stages):
        partial[stage] = total
        sums[stage, pl.ds(mine, 1), :] = total
        for i in range(1, count):
            pltpu.make_async_remote_copy(
                src_ref=partial.at[stage],
                dst_ref=sums.at[stage, pl.ds(mine, 1), :],
                send_sem=sum_send.at[stage],
                recv_sem=sum_recv.at[stage],
                device_id=device(lax.rem(mine + i, count)),
                device_id_type=MESH,
            ).start()
        got = sums.at[stage, pl.ds(0, count - 1), :]
        pltpu.make_async_copy(got, got, sum_recv.at[stage]).wait()
        total = jnp.sum(sums[stage, 0:count, :], axis=0, keepdims=True)
    total = jnp.sum(total, axis=1, keepdims=True)
    factor = jnp.minimum(1.0, 1.0 / jnp.sqrt(total / params + 1e-12))

    clipped = factor * trimmed[...]
    new_one = 0.9 * one_ref[...] + 0.1 * clipped
    new_two = 0.95 * two_ref[...] + 0.05 * clipped * clipped
    update = new_one / (1.0 - 0.9**STEP) / (jnp.sqrt(new_two / (1.0 - 0.95**STEP)) + 1e-08)
    owned = row[...]
    outgoing[...] = owned - 0.05 * (update + 0.1 * owned)
    new_one_ref[...] = new_one
    new_two_ref[...] = new_two

    first, last = pl.ds(0, SPLIT), pl.ds(SPLIT, 40 - SPLIT)
    right_left = (1, NX - 1)

    def part(r, tiles):
        return new_weight.at[:, r // 8, tiles, lax.rem(r, 8), :]

    def half(r, h):
        return new_weight.at[h, r // 8, first, lax.rem(r, 8), :]

    def four(zz):
        return new_weight.at[:, zz // 2, last, pl.ds(lax.rem(zz, 2) * 4, 4), :]

    def half_four(zz, h):
        return new_weight.at[h, zz // 2, last, pl.ds(lax.rem(zz, 2) * 4, 4), :]

    def push(src, dst, peer, sem):
        pltpu.make_async_remote_copy(
            src_ref=src,
            dst_ref=dst,
            send_sem=gather_send,
            recv_sem=sem,
            device_id=(peer, shard),
            device_id_type=MESH,
        ).start()

    def zs(dz):
        return lax.rem(z + dz, NZ)

    def along_x(dz, src=None):
        view = part(at(dz, 0), first)
        for side, dx in enumerate(right_left):
            push(view if src is None else src, view, at(0, dx), x_recv.at[side, zs(dz)])

    def relay_x(dz):
        for side, dx in enumerate(right_left):
            r = at(dz, NX - dx)
            came(part(r, first), x_recv.at[side, zs(dz)])
            push(half(r, side), half(r, side), at(0, dx), half_recv)

    def from_z(dz):
        came(part(at(dz, 0), first), z_recv.at[zs(dz)])

    own_first, own_last = outgoing.at[:, first, :], outgoing.at[:, last, :]
    for dz in (2, 6, 1, 7):
        push(own_first, part(me, first), at(dz, 0), z_recv.at[z])
    along_x(0, own_first)
    for dx in (2, 1, 3):
        push(own_last, part(me, last), at(0, dx), last_recv)
    keep = pltpu.make_async_copy(outgoing, row_of(new_weight, me), out_sem)
    keep.start()

    for dz in (1, 7):
        from_z(dz)
        along_x(dz)
    for dz, on in ((6, 1), (2, 7)):
        from_z(dz)
        r, h = at(dz, 0), (0 if on == 1 else 1)
        push(part(r, first), part(r, first), at(on, 0), z_recv.at[zs(dz)])
        push(half(r, h), half(r, h), at(2 * on % NZ, 0), z_recv.at[zs(dz)])
        along_x(dz)
    relay_x(0)
    three = received.at[pl.ds(0, 6), last, :]
    came(three, last_recv)
    keep.wait()
    for dz in (2, 6, 1, 7):
        push(four(z), four(z), at(dz, 0), four_recv.at[z])
    for dz in (1, 7, 2, 6):
        relay_x(dz)
    for dz in (3, 5, 4):
        from_z(dz)
        along_x(dz)
    for dz, on in ((6, 1), (2, 7)):
        zz, h = zs(dz), (0 if on == 1 else 1)
        came(four(zz), four_recv.at[zz])
        push(four(zz), four(zz), at(on, 0), four_recv.at[zz])
        push(half_four(zz, h), half_four(zz, h), at(2 * on % NZ, 0), four_recv.at[zz])
    for dz in (3, 5, 4):
        relay_x(dz)
    for dz in (1, 7, 3, 5, 4):
        came(four(zs(dz)), four_recv.at[zs(dz)])
    came(received.at[pl.ds(0, 16), first, :], half_recv)

    came(halves(60), send_sem)
    came(halves(18), summary_send)
    came(halves(62), gather_send)
    for stage, (count, _, _) in enumerate(stages):
        got = sums.at[stage, pl.ds(0, count - 1), :]
        pltpu.make_async_copy(got, got, sum_send.at[stage]).wait()


def store(*refs):
    *pairs, sems = refs
    copies = [pltpu.make_async_copy(pairs[i], pairs[i + 3], sems.at[i]) for i in range(3)]
    for copy in copies:
        copy.start()
    for copy in copies:
        copy.wait()


def pinned(array):
    return pltpu.with_memory_space_constraint(array, pltpu.HBM)


def on_device(grads, weight, moment_one, moment_two):
    params = weight.shape[0] * SHARDS * weight.shape[1] * weight.shape[2]
    vmem = pl.BlockSpec(memory_space=pltpu.VMEM)
    hbm = pl.BlockSpec(memory_space=pltpu.HBM)
    unit = (2, 40, 128)
    dma, regular = pltpu.SemaphoreType.DMA, pltpu.SemaphoreType.REGULAR
    results = pl.pallas_call(
        lambda *refs: kernel(params, *refs),
        name="robust_step",
        out_shape=(
            pltpu.VMEM((2, 4, 40, 8, 128), F32),
            pltpu.VMEM(unit, F32),
            pltpu.VMEM(unit, F32),
        ),
        in_specs=[hbm] * 4,
        out_specs=(vmem, vmem, vmem),
        scratch_shapes=[
            pltpu.VMEM((2 * REPS, 40, 128), F32),
            pltpu.VMEM((2, 9, 40, 128), F32),
            pltpu.VMEM(unit, F32),
            pltpu.VMEM(unit, F32),
            pltpu.VMEM(unit, F32),
            pltpu.VMEM(unit, F32),
            pltpu.VMEM(unit, F32),
            pltpu.VMEM((2, 1, 128), F32),
            pltpu.VMEM((2, 2 * REPS, 128), F32),
            dma((7,)),
            dma,
            dma((2,)),
            dma,
            dma,
            dma((2,)),
            dma((2,)),
            dma((2,)),
            dma,
            dma((NZ,)),
            dma((2, NZ)),
            dma,
            dma,
            dma((NZ,)),
            dma,
            regular((NZ,)),
            regular((NY // 2 - 1, 2)),
            regular,
        ],
        compiler_params=pltpu.CompilerParams(
            collective_id=0, has_side_effects=True, vmem_limit_bytes=32 << 20
        ),
    )(pinned(tiles(grads[0])), pinned(tiles(weight)), pinned(moment_one.reshape(unit)), pinned(moment_two.reshape(unit)))
    new_weight, new_one, new_two = pl.pallas_call(
        store,
        name="store",
        out_shape=tuple(jax.ShapeDtypeStruct(r.shape, F32) for r in results),
        in_specs=[vmem] * 3,
        out_specs=(hbm,) * 3,
        scratch_shapes=[dma((3,))],
        compiler_params=pltpu.CompilerParams(vmem_limit_bytes=16 << 20),
    )(*results)
    return (
        new_weight.transpose(0, 1, 3, 2, 4).reshape(weight.shape),
        new_one.reshape(moment_one.shape),
        new_two.reshape(moment_two.shape),
    )


def solution(mesh):
    return jax.shard_map(
        on_device,
        mesh=mesh,
        in_specs=(
            P("rep", "shard", None, None),
            P("shard", None, None),
            P("shard", "rep", None),
            P("shard", "rep", None),
        ),
        out_specs=(P("shard", None, None), P("shard", "rep", None), P("shard", "rep", None)),
        check_vma=False,
    )
```

```python
import jax
import jax.numpy as jnp
from jax import lax
from jax.experimental import pallas as pl
from jax.experimental.pallas import tpu as pltpu
from jax.sharding import PartitionSpec as P

STEP = 100
MESH = pl.DeviceIdType.MESH
NZ, NX, NY = 8, 4, 8
REPS, SHARDS = 32, 16
TRIM = 4
SPLIT = 24
F32 = jnp.float32

SORT8 = (
    (0, 1), (2, 3), (4, 5), (6, 7),
    (0, 2), (1, 3), (4, 6), (5, 7),
    (1, 2), (5, 6),
    (0, 4), (1, 5), (2, 6), (3, 7),
    (2, 4), (3, 5),
    (1, 2), (3, 4), (5, 6),
)


def exchange(values, i, j):
    a, b = values[i], values[j]
    values[i], values[j] = jnp.minimum(a, b), jnp.maximum(a, b)


def sort8(values):
    values = list(values)
    for i, j in SORT8:
        exchange(values, i, j)
    return values[:4], values[4:]


def add_all(values):
    values = list(values)
    while len(values) > 1:
        values = [a + b for a, b in zip(values[::2], values[1::2])] + (
            [values[-1]] if len(values) % 2 else []
        )
    return values[0]


def merge(one, two):
    (low_a, high_a), (low_b, high_b) = one, two
    low = [jnp.minimum(low_a[i], low_b[3 - i]) for i in range(4)]
    high = [jnp.maximum(high_a[i], high_b[3 - i]) for i in range(4)]
    for i, j in ((0, 2), (1, 3), (0, 1), (2, 3)):
        exchange(low, i, j)
        exchange(high, i, j)
    return (low, high), middle(one, two)


def middle(one, two):
    (low_a, high_a), (low_b, high_b) = one, two
    return add_all(
        [jnp.maximum(low_a[i], low_b[3 - i]) for i in range(4)]
        + [jnp.minimum(high_a[i], high_b[3 - i]) for i in range(4)]
    )


def row_of(ref, r):
    return ref.at[:, r // 8, :, lax.rem(r, 8), :]


def half_row(ref, r, h):
    return ref.at[h, r // 8, :, lax.rem(r, 8), :]


def bundle(h, slot):
    return h * 16 + slot


def direct(h, slot):
    return REPS + h * 16 + slot


def tiles(block):
    return block.reshape(2, 4, 8, 40, 128).transpose(0, 1, 3, 2, 4)


def kernel(
    params,
    grads,
    weight,
    moment_one,
    moment_two,
    new_weight,
    new_one_ref,
    new_two_ref,
    received,
    summary,
    row,
    one_ref,
    two_ref,
    outgoing,
    trimmed,
    partial,
    sums,
    local_sem,
    send_sem,
    bundle_recv,
    recv_sem,
    summary_send,
    summary_recv,
    sum_send,
    sum_recv,
    gather_send,
    z_recv,
    x_recv,
    half_recv,
    last_recv,
    four_recv,
    out_sem,
    above_sem,
    ring_sem,
    core_sem,
):
    me = lax.axis_index("rep")
    shard = lax.axis_index("shard")
    z, x = me // NX, lax.rem(me, NX)

    def at(dz, dx):
        return lax.rem(z + dz, NZ) * NX + lax.rem(x + dx, NX)

    y, core = shard // 2, lax.rem(shard, 2)

    def in_y(dy):
        return lax.rem(y + dy, NY) * 2 + core

    local = [
        pltpu.make_async_copy(src, dst, local_sem.at[i])
        for i, (src, dst) in enumerate(
            (
                (half_row(grads, me, 0), received.at[direct(0, x)]),
                (half_row(grads, me, 1), received.at[direct(1, x)]),
                (half_row(grads, at(NZ - 1, 0), 0), received.at[bundle(0, x)]),
                (half_row(grads, at(1, 0), 1), received.at[bundle(1, x)]),
                (row_of(weight, me), row),
                (moment_one, one_ref),
                (moment_two, two_ref),
            )
        )
    ]

    barrier = pltpu.get_barrier_semaphore()

    def signal(sem, rep, sh):
        pl.semaphore_signal(sem, inc=1, device_id=(rep, sh), device_id_type=MESH)

    for dx in (2, 1, 3):
        signal(barrier, at(0, dx), shard)
    for dy in (1, NY - 1):
        signal(barrier, me, in_y(dy))

    @pl.when(core == 0)
    def _():
        signal(barrier, me, shard + 1)

    @pl.loop(z + 1, NZ)
    def _(zz):
        for xx in range(NX):
            signal(barrier, zz * NX + xx, shard)

    pl.semaphore_wait(barrier, 5 + NX * z + core)

    @pl.loop(0, z)
    def _(zz):
        signal(above_sem.at[z], zz * NX + x, shard)

    def send_half(row_index, h, slot, peer, sem):
        pltpu.make_async_remote_copy(
            src_ref=half_row(grads, row_index, h),
            dst_ref=received.at[slot],
            send_sem=send_sem,
            recv_sem=sem,
            device_id=(peer, shard),
            device_id_type=MESH,
        ).start()

    def towards(zz):
        d = lax.rem(zz - z + NZ, NZ)
        down = (d > NZ // 2).astype(jnp.int32)
        distance = d + down * (NZ - 2 * d)
        return down, distance, d != NZ // 2

    def send_bundles(zz):
        down, distance, far = towards(zz)
        beyond = lax.rem(zz + 1 + down * (NZ - 2), NZ)

        @pl.when(far)
        def _():
            for dx in (2, 1, 3, 0):
                xx = lax.rem(x + dx, NX)
                slot = bundle(1 - down, distance * NX + x)
                send_half(beyond * NX + xx, 1 - down, slot, zz * NX + xx, bundle_recv.at[1 - down])

    def send_direct(zz):
        down, distance, far = towards(zz)

        @pl.when(far)
        def _():
            for dx in (2, 1, 3, 0):
                xx = lax.rem(x + dx, NX)
                slot = direct(down, distance * NX + x)
                send_half(zz * NX + xx, down, slot, zz * NX + xx, recv_sem)

    pl.loop(0, z)(send_bundles)

    for dx in (2, 1, 3):
        send_half(at(NZ - 1, dx), 0, bundle(0, x), at(0, dx), bundle_recv.at[0])
        send_half(at(1, dx), 1, bundle(1, x), at(0, dx), bundle_recv.at[1])

    pl.loop(0, z)(send_direct)

    for dx in (2, 1, 3):
        for h in range(2):
            send_half(at(0, dx), h, direct(h, x), at(0, dx), recv_sem)

    @pl.loop(z + 1, NZ)
    def _(zz):
        pl.semaphore_wait(above_sem.at[zz], 1)
        send_bundles(zz)

    pl.loop(z + 1, NZ)(send_direct)

    for copy in local:
        copy.start()

    @pl.when(core == 0)
    def _():
        pl.semaphore_wait(core_sem, 1)

    signal(core_sem, me, shard + 1 - 2 * core)

    @pl.when(core == 1)
    def _():
        pl.semaphore_wait(core_sem, 1)

    for r in range(NY // 2 - 1):
        for side, dy in enumerate((1, NY - 1)):
            signal(ring_sem.at[r, side], me, in_y(dy))
        for side in range(2):
            pl.semaphore_wait(ring_sem.at[r, side], 1)

    for copy in local:
        copy.wait()
    def came(view, sem):
        pltpu.make_async_copy(view, view, sem).wait()

    def halves(n):
        return received.at[pl.ds(0, n)]

    def condense(first_slot):
        @pl.loop(0, 5)
        def _(j):
            rows = pl.ds(pl.multiple_of(j * 8, 8), 8)
            values = [received[first_slot + i, rows, :] for i in range(16)]
            (low, high), rest = merge(sort8(values[:8]), sort8(values[8:]))
            for i, value in enumerate(low + high + [rest]):
                received[first_slot + i, rows, :] = value

    for h, dz in enumerate((NZ - 1, 1)):
        came(halves(15), bundle_recv.at[h])
        condense(bundle(h, 0))
        pltpu.make_async_remote_copy(
            src_ref=received.at[pl.ds(bundle(h, 0), 9)],
            dst_ref=summary.at[h],
            send_sem=summary_send,
            recv_sem=summary_recv.at[h],
            device_id=(at(dz, 0), shard),
            device_id_type=MESH,
        ).start()
    came(halves(30), recv_sem)
    for h in range(2):
        condense(direct(h, 0))
    for h in range(2):
        came(halves(9), summary_recv.at[h])

    def block(j, squares):
        h, rows = j // 5, pl.ds(pl.multiple_of(lax.rem(j, 5) * 8, 8), 8)
        near = [received[direct(h, i), rows, :] for i in range(9)]
        far = [summary[h, i, rows, :] for i in range(9)]
        rest = middle((near[:4], near[4:8]), (far[:4], far[4:8]))
        mean = (near[8] + far[8] + rest) / (REPS - 2 * TRIM)
        trimmed[h, rows, :] = mean
        return squares + mean * mean

    squares = lax.fori_loop(0, 10, block, jnp.zeros((8, 128), F32))
    total = jnp.sum(squares, axis=0, keepdims=True)

    stages = (
        (2 * REPS, me * 2 + core, lambda p: (p // 2, y * 2 + lax.rem(p, 2))),
        (NY, y, lambda p: (me, p * 2 + core)),
    )
    for stage, (count, mine, device) in enumerate(stages):
        partial[stage] = total
        sums[stage, pl.ds(mine, 1), :] = total
        for i in range(1, count):
            pltpu.make_async_remote_copy(
                src_ref=partial.at[stage],
                dst_ref=sums.at[stage, pl.ds(mine, 1), :],
                send_sem=sum_send.at[stage],
                recv_sem=sum_recv.at[stage],
                device_id=device(lax.rem(mine + i, count)),
                device_id_type=MESH,
            ).start()
        got = sums.at[stage, pl.ds(0, count - 1), :]
        pltpu.make_async_copy(got, got, sum_recv.at[stage]).wait()
        total = jnp.sum(sums[stage, 0:count, :], axis=0, keepdims=True)
    total = jnp.sum(total, axis=1, keepdims=True)
    factor = jnp.minimum(1.0, 1.0 / jnp.sqrt(total / params + 1e-12))

    clipped = factor * trimmed[...]
    new_one = 0.9 * one_ref[...] + 0.1 * clipped
    new_two = 0.95 * two_ref[...] + 0.05 * clipped * clipped
    update = new_one / (1.0 - 0.9**STEP) / (jnp.sqrt(new_two / (1.0 - 0.95**STEP)) + 1e-08)
    owned = row[...]
    outgoing[...] = owned - 0.05 * (update + 0.1 * owned)
    new_one_ref[...] = new_one
    new_two_ref[...] = new_two

    first, last = pl.ds(0, SPLIT), pl.ds(SPLIT, 40 - SPLIT)
    right_left = (1, NX - 1)

    def part(r, tiles):
        return new_weight.at[:, r // 8, tiles, lax.rem(r, 8), :]

    def half(r, h):
        return new_weight.at[h, r // 8, first, lax.rem(r, 8), :]

    def four(zz):
        return new_weight.at[:, zz // 2, last, pl.ds(lax.rem(zz, 2) * 4, 4), :]

    def half_four(zz, h):
        return new_weight.at[h, zz // 2, last, pl.ds(lax.rem(zz, 2) * 4, 4), :]

    def push(src, dst, peer, sem):
        pltpu.make_async_remote_copy(
            src_ref=src,
            dst_ref=dst,
            send_sem=gather_send,
            recv_sem=sem,
            device_id=(peer, shard),
            device_id_type=MESH,
        ).start()

    def zs(dz):
        return lax.rem(z + dz, NZ)

    def along_x(dz, src=None):
        view = part(at(dz, 0), first)
        for side, dx in enumerate(right_left):
            push(view if src is None else src, view, at(0, dx), x_recv.at[side, zs(dz)])

    def relay_x(dz):
        for side, dx in enumerate(right_left):
            r = at(dz, NX - dx)
            came(part(r, first), x_recv.at[side, zs(dz)])
            push(half(r, side), half(r, side), at(0, dx), half_recv)

    def from_z(dz):
        came(part(at(dz, 0), first), z_recv.at[zs(dz)])

    own_first, own_last = outgoing.at[:, first, :], outgoing.at[:, last, :]
    for dz in (2, 6, 1, 7):
        push(own_first, part(me, first), at(dz, 0), z_recv.at[z])
    along_x(0, own_first)
    for dx in (2, 1, 3):
        push(own_last, part(me, last), at(0, dx), last_recv)
    keep = pltpu.make_async_copy(outgoing, row_of(new_weight, me), out_sem)
    keep.start()

    for dz in (1, 7):
        from_z(dz)
        along_x(dz)
    for dz, on in ((6, 1), (2, 7)):
        from_z(dz)
        r, h = at(dz, 0), (0 if on == 1 else 1)
        push(part(r, first), part(r, first), at(on, 0), z_recv.at[zs(dz)])
        push(half(r, h), half(r, h), at(2 * on % NZ, 0), z_recv.at[zs(dz)])
        along_x(dz)
    relay_x(0)
    three = received.at[pl.ds(0, 6), last, :]
    came(three, last_recv)
    keep.wait()
    for dz in (2, 6, 1, 7):
        push(four(z), four(z), at(dz, 0), four_recv.at[z])
    for dz in (1, 7, 2, 6):
        relay_x(dz)
    for dz in (3, 5, 4):
        from_z(dz)
        along_x(dz)
    for dz, on in ((6, 1), (2, 7)):
        zz, h = zs(dz), (0 if on == 1 else 1)
        came(four(zz), four_recv.at[zz])
        push(four(zz), four(zz), at(on, 0), four_recv.at[zz])
        push(half_four(zz, h), half_four(zz, h), at(2 * on % NZ, 0), four_recv.at[zz])
    for dz in (3, 5, 4):
        relay_x(dz)
    for dz in (1, 7, 3, 5, 4):
        came(four(zs(dz)), four_recv.at[zs(dz)])
    came(received.at[pl.ds(0, 16), first, :], half_recv)

    came(halves(60), send_sem)
    came(halves(18), summary_send)
    came(halves(62), gather_send)
    for stage, (count, _, _) in enumerate(stages):
        got = sums.at[stage, pl.ds(0, count - 1), :]
        pltpu.make_async_copy(got, got, sum_send.at[stage]).wait()


def store(*refs):
    *pairs, sems = refs
    copies = [pltpu.make_async_copy(pairs[i], pairs[i + 3], sems.at[i]) for i in range(3)]
    for copy in copies:
        copy.start()
    for copy in copies:
        copy.wait()


def pinned(array):
    return pltpu.with_memory_space_constraint(array, pltpu.HBM)


def on_device(grads, weight, moment_one, moment_two):
    params = weight.shape[0] * SHARDS * weight.shape[1] * weight.shape[2]
    vmem = pl.BlockSpec(memory_space=pltpu.VMEM)
    hbm = pl.BlockSpec(memory_space=pltpu.HBM)
    unit = (2, 40, 128)
    dma, regular = pltpu.SemaphoreType.DMA, pltpu.SemaphoreType.REGULAR
    results = pl.pallas_call(
        lambda *refs: kernel(params, *refs),
        name="robust_step",
        out_shape=(
            pltpu.VMEM((2, 4, 40, 8, 128), F32),
            pltpu.VMEM(unit, F32),
            pltpu.VMEM(unit, F32),
        ),
        in_specs=[hbm] * 4,
        out_specs=(vmem, vmem, vmem),
        scratch_shapes=[
            pltpu.VMEM((2 * REPS, 40, 128), F32),
            pltpu.VMEM((2, 9, 40, 128), F32),
            pltpu.VMEM(unit, F32),
            pltpu.VMEM(unit, F32),
            pltpu.VMEM(unit, F32),
            pltpu.VMEM(unit, F32),
            pltpu.VMEM(unit, F32),
            pltpu.VMEM((2, 1, 128), F32),
            pltpu.VMEM((2, 2 * REPS, 128), F32),
            dma((7,)),
            dma,
            dma((2,)),
            dma,
            dma,
            dma((2,)),
            dma((2,)),
            dma((2,)),
            dma,
            dma((NZ,)),
            dma((2, NZ)),
            dma,
            dma,
            dma((NZ,)),
            dma,
            regular((NZ,)),
            regular((NY // 2 - 1, 2)),
            regular,
        ],
        compiler_params=pltpu.CompilerParams(
            collective_id=0, has_side_effects=True, vmem_limit_bytes=32 << 20
        ),
    )(pinned(tiles(grads[0])), pinned(tiles(weight)), pinned(moment_one.reshape(unit)), pinned(moment_two.reshape(unit)))
    new_weight, new_one, new_two = pl.pallas_call(
        store,
        name="store",
        out_shape=tuple(jax.ShapeDtypeStruct(r.shape, F32) for r in results),
        in_specs=[vmem] * 3,
        out_specs=(hbm,) * 3,
        scratch_shapes=[dma((3,))],
        compiler_params=pltpu.CompilerParams(vmem_limit_bytes=16 << 20),
    )(*results)
    return (
        new_weight.transpose(0, 1, 3, 2, 4).reshape(weight.shape),
        new_one.reshape(moment_one.shape),
        new_two.reshape(moment_two.shape),
    )


def solution(mesh):
    return jax.shard_map(
        on_device,
        mesh=mesh,
        in_specs=(
            P("rep", "shard", None, None),
            P("shard", None, None),
            P("shard", "rep", None),
            P("shard", "rep", None),
        ),
        out_specs=(P("shard", None, None), P("shard", "rep", None), P("shard", "rep", None)),
        check_vma=False,
    )
```

```python
import jax
import jax.numpy as jnp
from jax import lax
from jax.experimental import pallas as pl
from jax.experimental.pallas import tpu as pltpu
from jax.sharding import PartitionSpec as P

STEP = 100
MESH = pl.DeviceIdType.MESH
NZ, NX, NY = 8, 4, 8
REPS, SHARDS = 32, 16
TRIM = 4
SPLIT = 24
F32 = jnp.float32

SORT8 = (
    (0, 1), (2, 3), (4, 5), (6, 7),
    (0, 2), (1, 3), (4, 6), (5, 7),
    (1, 2), (5, 6),
    (0, 4), (1, 5), (2, 6), (3, 7),
    (2, 4), (3, 5),
    (1, 2), (3, 4), (5, 6),
)


def exchange(values, i, j):
    a, b = values[i], values[j]
    values[i], values[j] = jnp.minimum(a, b), jnp.maximum(a, b)


def sort8(values):
    values = list(values)
    for i, j in SORT8:
        exchange(values, i, j)
    return values[:4], values[4:]


def add_all(values):
    values = list(values)
    while len(values) > 1:
        values = [a + b for a, b in zip(values[::2], values[1::2])] + (
            [values[-1]] if len(values) % 2 else []
        )
    return values[0]


def merge(one, two):
    (low_a, high_a), (low_b, high_b) = one, two
    low = [jnp.minimum(low_a[i], low_b[3 - i]) for i in range(4)]
    high = [jnp.maximum(high_a[i], high_b[3 - i]) for i in range(4)]
    for i, j in ((0, 2), (1, 3), (0, 1), (2, 3)):
        exchange(low, i, j)
        exchange(high, i, j)
    return (low, high), middle(one, two)


def middle(one, two):
    (low_a, high_a), (low_b, high_b) = one, two
    return add_all(
        [jnp.maximum(low_a[i], low_b[3 - i]) for i in range(4)]
        + [jnp.minimum(high_a[i], high_b[3 - i]) for i in range(4)]
    )


def row_of(ref, r):
    return ref.at[:, r // 8, :, lax.rem(r, 8), :]


def half_row(ref, r, h):
    return ref.at[h, r // 8, :, lax.rem(r, 8), :]


def bundle(h, slot):
    return h * 16 + slot


def direct(h, slot):
    return REPS + h * 16 + slot


def tiles(block):
    return block.reshape(2, 4, 8, 40, 128).transpose(0, 1, 3, 2, 4)


def kernel(
    params,
    grads,
    weight,
    moment_one,
    moment_two,
    new_weight,
    new_one_ref,
    new_two_ref,
    received,
    summary,
    row,
    one_ref,
    two_ref,
    outgoing,
    trimmed,
    partial,
    sums,
    local_sem,
    send_sem,
    bundle_recv,
    recv_sem,
    summary_send,
    summary_recv,
    sum_send,
    sum_recv,
    gather_send,
    z_recv,
    x_recv,
    half_recv,
    last_recv,
    four_recv,
    out_sem,
    above_sem,
    ring_sem,
    core_sem,
):
    me = lax.axis_index("rep")
    shard = lax.axis_index("shard")
    z, x = me // NX, lax.rem(me, NX)

    def at(dz, dx):
        return lax.rem(z + dz, NZ) * NX + lax.rem(x + dx, NX)

    y, core = shard // 2, lax.rem(shard, 2)

    def in_y(dy):
        return lax.rem(y + dy, NY) * 2 + core

    local = [
        pltpu.make_async_copy(src, dst, local_sem.at[i])
        for i, (src, dst) in enumerate(
            (
                (half_row(grads, me, 0), received.at[direct(0, x)]),
                (half_row(grads, me, 1), received.at[direct(1, x)]),
                (half_row(grads, at(NZ - 1, 0), 0), received.at[bundle(0, x)]),
                (half_row(grads, at(1, 0), 1), received.at[bundle(1, x)]),
                (row_of(weight, me), row),
                (moment_one, one_ref),
                (moment_two, two_ref),
            )
        )
    ]

    barrier = pltpu.get_barrier_semaphore()

    def signal(sem, rep, sh):
        pl.semaphore_signal(sem, inc=1, device_id=(rep, sh), device_id_type=MESH)

    for dx in (2, 1, 3):
        signal(barrier, at(0, dx), shard)
    for dy in (1, NY - 1):
        signal(barrier, me, in_y(dy))

    @pl.when(core == 0)
    def _():
        signal(barrier, me, shard + 1)

    @pl.loop(z + 1, NZ)
    def _(zz):
        for xx in range(NX):
            signal(barrier, zz * NX + xx, shard)

    pl.semaphore_wait(barrier, 5 + NX * z + core)

    @pl.loop(0, z)
    def _(zz):
        signal(above_sem.at[z], zz * NX + x, shard)

    def send_half(row_index, h, slot, peer, sem):
        pltpu.make_async_remote_copy(
            src_ref=half_row(grads, row_index, h),
            dst_ref=received.at[slot],
            send_sem=send_sem,
            recv_sem=sem,
            device_id=(peer, shard),
            device_id_type=MESH,
        ).start()

    def towards(zz):
        d = lax.rem(zz - z + NZ, NZ)
        down = (d > NZ // 2).astype(jnp.int32)
        distance = d + down * (NZ - 2 * d)
        return down, distance, d != NZ // 2

    def send_bundles(zz):
        down, distance, far = towards(zz)
        beyond = lax.rem(zz + 1 + down * (NZ - 2), NZ)

        @pl.when(far)
        def _():
            for dx in (2, 1, 3, 0):
                xx = lax.rem(x + dx, NX)
                slot = bundle(1 - down, distance * NX + x)
                send_half(beyond * NX + xx, 1 - down, slot, zz * NX + xx, bundle_recv.at[1 - down])

    def send_direct(zz):
        down, distance, far = towards(zz)

        @pl.when(far)
        def _():
            for dx in (2, 1, 3, 0):
                xx = lax.rem(x + dx, NX)
                slot = direct(down, distance * NX + x)
                send_half(zz * NX + xx, down, slot, zz * NX + xx, recv_sem)

    pl.loop(0, z)(send_bundles)

    for dx in (2, 1, 3):
        send_half(at(NZ - 1, dx), 0, bundle(0, x), at(0, dx), bundle_recv.at[0])
        send_half(at(1, dx), 1, bundle(1, x), at(0, dx), bundle_recv.at[1])

    pl.loop(0, z)(send_direct)

    for dx in (2, 1, 3):
        for h in range(2):
            send_half(at(0, dx), h, direct(h, x), at(0, dx), recv_sem)

    @pl.loop(z + 1, NZ)
    def _(zz):
        pl.semaphore_wait(above_sem.at[zz], 1)
        send_bundles(zz)

        @pl.when(zz - 1 > z)
        def _():
            send_direct(zz - 1)

    pl.loop(jnp.maximum(z + 1, NZ - 1), NZ)(send_direct)

    for copy in local:
        copy.start()

    @pl.when(core == 0)
    def _():
        pl.semaphore_wait(core_sem, 1)

    signal(core_sem, me, shard + 1 - 2 * core)

    @pl.when(core == 1)
    def _():
        pl.semaphore_wait(core_sem, 1)

    for r in range(NY // 2 - 1):
        for side, dy in enumerate((1, NY - 1)):
            signal(ring_sem.at[r, side], me, in_y(dy))
        for side in range(2):
            pl.semaphore_wait(ring_sem.at[r, side], 1)

    for copy in local:
        copy.wait()
    def came(view, sem):
        pltpu.make_async_copy(view, view, sem).wait()

    def halves(n):
        return received.at[pl.ds(0, n)]

    def condense(first_slot):
        @pl.loop(0, 5)
        def _(j):
            rows = pl.ds(pl.multiple_of(j * 8, 8), 8)
            values = [received[first_slot + i, rows, :] for i in range(16)]
            (low, high), rest = merge(sort8(values[:8]), sort8(values[8:]))
            for i, value in enumerate(low + high + [rest]):
                received[first_slot + i, rows, :] = value

    for h, dz in enumerate((NZ - 1, 1)):
        came(halves(15), bundle_recv.at[h])
        condense(bundle(h, 0))
        pltpu.make_async_remote_copy(
            src_ref=received.at[pl.ds(bundle(h, 0), 9)],
            dst_ref=summary.at[h],
            send_sem=summary_send,
            recv_sem=summary_recv.at[h],
            device_id=(at(dz, 0), shard),
            device_id_type=MESH,
        ).start()
    came(halves(30), recv_sem)
    for h in range(2):
        condense(direct(h, 0))
    for h in range(2):
        came(halves(9), summary_recv.at[h])

    def block(j, squares):
        h, rows = j // 5, pl.ds(pl.multiple_of(lax.rem(j, 5) * 8, 8), 8)
        near = [received[direct(h, i), rows, :] for i in range(9)]
        far = [summary[h, i, rows, :] for i in range(9)]
        rest = middle((near[:4], near[4:8]), (far[:4], far[4:8]))
        mean = (near[8] + far[8] + rest) / (REPS - 2 * TRIM)
        trimmed[h, rows, :] = mean
        return squares + mean * mean

    squares = lax.fori_loop(0, 10, block, jnp.zeros((8, 128), F32))
    total = jnp.sum(squares, axis=0, keepdims=True)

    stages = (
        (2 * REPS, me * 2 + core, lambda p: (p // 2, y * 2 + lax.rem(p, 2))),
        (NY, y, lambda p: (me, p * 2 + core)),
    )
    for stage, (count, mine, device) in enumerate(stages):
        partial[stage] = total
        sums[stage, pl.ds(mine, 1), :] = total
        for i in range(1, count):
            pltpu.make_async_remote_copy(
                src_ref=partial.at[stage],
                dst_ref=sums.at[stage, pl.ds(mine, 1), :],
                send_sem=sum_send.at[stage],
                recv_sem=sum_recv.at[stage],
                device_id=device(lax.rem(mine + i, count)),
                device_id_type=MESH,
            ).start()
        got = sums.at[stage, pl.ds(0, count - 1), :]
        pltpu.make_async_copy(got, got, sum_recv.at[stage]).wait()
        total = jnp.sum(sums[stage, 0:count, :], axis=0, keepdims=True)
    total = jnp.sum(total, axis=1, keepdims=True)
    factor = jnp.minimum(1.0, 1.0 / jnp.sqrt(total / params + 1e-12))

    clipped = factor * trimmed[...]
    new_one = 0.9 * one_ref[...] + 0.1 * clipped
    new_two = 0.95 * two_ref[...] + 0.05 * clipped * clipped
    update = new_one / (1.0 - 0.9**STEP) / (jnp.sqrt(new_two / (1.0 - 0.95**STEP)) + 1e-08)
    owned = row[...]
    outgoing[...] = owned - 0.05 * (update + 0.1 * owned)
    new_one_ref[...] = new_one
    new_two_ref[...] = new_two

    first, last = pl.ds(0, SPLIT), pl.ds(SPLIT, 40 - SPLIT)
    right_left = (1, NX - 1)

    def part(r, tiles):
        return new_weight.at[:, r // 8, tiles, lax.rem(r, 8), :]

    def half(r, h):
        return new_weight.at[h, r // 8, first, lax.rem(r, 8), :]

    def four(zz):
        return new_weight.at[:, zz // 2, last, pl.ds(lax.rem(zz, 2) * 4, 4), :]

    def half_four(zz, h):
        return new_weight.at[h, zz // 2, last, pl.ds(lax.rem(zz, 2) * 4, 4), :]

    def push(src, dst, peer, sem):
        pltpu.make_async_remote_copy(
            src_ref=src,
            dst_ref=dst,
            send_sem=gather_send,
            recv_sem=sem,
            device_id=(peer, shard),
            device_id_type=MESH,
        ).start()

    def zs(dz):
        return lax.rem(z + dz, NZ)

    def along_x(dz, src=None):
        view = part(at(dz, 0), first)
        for side, dx in enumerate(right_left):
            push(view if src is None else src, view, at(0, dx), x_recv.at[side, zs(dz)])

    def relay_x(dz):
        for side, dx in enumerate(right_left):
            r = at(dz, NX - dx)
            came(part(r, first), x_recv.at[side, zs(dz)])
            push(half(r, side), half(r, side), at(0, dx), half_recv)

    def from_z(dz):
        came(part(at(dz, 0), first), z_recv.at[zs(dz)])

    own_first, own_last = outgoing.at[:, first, :], outgoing.at[:, last, :]
    for dz in (2, 6, 1, 7):
        push(own_first, part(me, first), at(dz, 0), z_recv.at[z])
    along_x(0, own_first)
    for dx in (2, 1, 3):
        push(own_last, part(me, last), at(0, dx), last_recv)
    keep = pltpu.make_async_copy(outgoing, row_of(new_weight, me), out_sem)
    keep.start()

    for dz in (1, 7):
        from_z(dz)
        along_x(dz)
    for dz, on in ((6, 1), (2, 7)):
        from_z(dz)
        r, h = at(dz, 0), (0 if on == 1 else 1)
        push(part(r, first), part(r, first), at(on, 0), z_recv.at[zs(dz)])
        push(half(r, h), half(r, h), at(2 * on % NZ, 0), z_recv.at[zs(dz)])
        along_x(dz)
    relay_x(0)
    three = received.at[pl.ds(0, 6), last, :]
    came(three, last_recv)
    keep.wait()
    for dz in (2, 6, 1, 7):
        push(four(z), four(z), at(dz, 0), four_recv.at[z])
    for dz in (3, 5, 4):
        from_z(dz)
        along_x(dz)
    for dz in (1, 7, 2, 6):
        relay_x(dz)
    for dz, on in ((6, 1), (2, 7)):
        zz, h = zs(dz), (0 if on == 1 else 1)
        came(four(zz), four_recv.at[zz])
        push(four(zz), four(zz), at(on, 0), four_recv.at[zz])
        push(half_four(zz, h), half_four(zz, h), at(2 * on % NZ, 0), four_recv.at[zz])
    for dz in (3, 5, 4):
        relay_x(dz)
    for dz in (1, 7, 3, 5, 4):
        came(four(zs(dz)), four_recv.at[zs(dz)])
    came(received.at[pl.ds(0, 16), first, :], half_recv)

    came(halves(60), send_sem)
    came(halves(18), summary_send)
    came(halves(62), gather_send)
    for stage, (count, _, _) in enumerate(stages):
        got = sums.at[stage, pl.ds(0, count - 1), :]
        pltpu.make_async_copy(got, got, sum_send.at[stage]).wait()


def store(*refs):
    *pairs, sems = refs
    copies = [pltpu.make_async_copy(pairs[i], pairs[i + 3], sems.at[i]) for i in range(3)]
    for copy in copies:
        copy.start()
    for copy in copies:
        copy.wait()


def pinned(array):
    return pltpu.with_memory_space_constraint(array, pltpu.HBM)


def on_device(grads, weight, moment_one, moment_two):
    params = weight.shape[0] * SHARDS * weight.shape[1] * weight.shape[2]
    vmem = pl.BlockSpec(memory_space=pltpu.VMEM)
    hbm = pl.BlockSpec(memory_space=pltpu.HBM)
    unit = (2, 40, 128)
    dma, regular = pltpu.SemaphoreType.DMA, pltpu.SemaphoreType.REGULAR
    results = pl.pallas_call(
        lambda *refs: kernel(params, *refs),
        name="robust_step",
        out_shape=(
            pltpu.VMEM((2, 4, 40, 8, 128), F32),
            pltpu.VMEM(unit, F32),
            pltpu.VMEM(unit, F32),
        ),
        in_specs=[hbm] * 4,
        out_specs=(vmem, vmem, vmem),
        scratch_shapes=[
            pltpu.VMEM((2 * REPS, 40, 128), F32),
            pltpu.VMEM((2, 9, 40, 128), F32),
            pltpu.VMEM(unit, F32),
            pltpu.VMEM(unit, F32),
            pltpu.VMEM(unit, F32),
            pltpu.VMEM(unit, F32),
            pltpu.VMEM(unit, F32),
            pltpu.VMEM((2, 1, 128), F32),
            pltpu.VMEM((2, 2 * REPS, 128), F32),
            dma((7,)),
            dma,
            dma((2,)),
            dma,
            dma,
            dma((2,)),
            dma((2,)),
            dma((2,)),
            dma,
            dma((NZ,)),
            dma((2, NZ)),
            dma,
            dma,
            dma((NZ,)),
            dma,
            regular((NZ,)),
            regular((NY // 2 - 1, 2)),
            regular,
        ],
        compiler_params=pltpu.CompilerParams(
            collective_id=0, has_side_effects=True, vmem_limit_bytes=32 << 20
        ),
    )(pinned(tiles(grads[0])), pinned(tiles(weight)), pinned(moment_one.reshape(unit)), pinned(moment_two.reshape(unit)))
    new_weight, new_one, new_two = pl.pallas_call(
        store,
        name="store",
        out_shape=tuple(jax.ShapeDtypeStruct(r.shape, F32) for r in results),
        in_specs=[vmem] * 3,
        out_specs=(hbm,) * 3,
        scratch_shapes=[dma((3,))],
        compiler_params=pltpu.CompilerParams(vmem_limit_bytes=16 << 20),
    )(*results)
    return (
        new_weight.transpose(0, 1, 3, 2, 4).reshape(weight.shape),
        new_one.reshape(moment_one.shape),
        new_two.reshape(moment_two.shape),
    )


def solution(mesh):
    return jax.shard_map(
        on_device,
        mesh=mesh,
        in_specs=(
            P("rep", "shard", None, None),
            P("shard", None, None),
            P("shard", "rep", None),
            P("shard", "rep", None),
        ),
        out_specs=(P("shard", None, None), P("shard", "rep", None), P("shard", "rep", None)),
        check_vma=False,
    )
```

```python
import jax
import jax.numpy as jnp
from jax import lax
from jax.experimental import pallas as pl
from jax.experimental.pallas import tpu as pltpu
from jax.sharding import PartitionSpec as P

STEP = 100
MESH = pl.DeviceIdType.MESH
NZ, NX, NY = 8, 4, 8
REPS, SHARDS = 32, 16
TRIM = 4
SPLIT = 24
F32 = jnp.float32

SORT8 = (
    (0, 1), (2, 3), (4, 5), (6, 7),
    (0, 2), (1, 3), (4, 6), (5, 7),
    (1, 2), (5, 6),
    (0, 4), (1, 5), (2, 6), (3, 7),
    (2, 4), (3, 5),
    (1, 2), (3, 4), (5, 6),
)


def exchange(values, i, j):
    a, b = values[i], values[j]
    values[i], values[j] = jnp.minimum(a, b), jnp.maximum(a, b)


def sort8(values):
    values = list(values)
    for i, j in SORT8:
        exchange(values, i, j)
    return values[:4], values[4:]


def add_all(values):
    values = list(values)
    while len(values) > 1:
        values = [a + b for a, b in zip(values[::2], values[1::2])] + (
            [values[-1]] if len(values) % 2 else []
        )
    return values[0]


def merge(one, two):
    (low_a, high_a), (low_b, high_b) = one, two
    low = [jnp.minimum(low_a[i], low_b[3 - i]) for i in range(4)]
    high = [jnp.maximum(high_a[i], high_b[3 - i]) for i in range(4)]
    for i, j in ((0, 2), (1, 3), (0, 1), (2, 3)):
        exchange(low, i, j)
        exchange(high, i, j)
    return (low, high), middle(one, two)


def middle(one, two):
    (low_a, high_a), (low_b, high_b) = one, two
    return add_all(
        [jnp.maximum(low_a[i], low_b[3 - i]) for i in range(4)]
        + [jnp.minimum(high_a[i], high_b[3 - i]) for i in range(4)]
    )


def row_of(ref, r):
    return ref.at[:, r // 8, :, lax.rem(r, 8), :]


def half_row(ref, r, h):
    return ref.at[h, r // 8, :, lax.rem(r, 8), :]


def bundle(h, slot):
    return h * 16 + slot


def direct(h, slot):
    return REPS + h * 16 + slot


def tiles(block):
    return block.reshape(2, 4, 8, 40, 128).transpose(0, 1, 3, 2, 4)


def kernel(
    params,
    grads,
    weight,
    moment_one,
    moment_two,
    new_weight,
    new_one_ref,
    new_two_ref,
    received,
    summary,
    row,
    one_ref,
    two_ref,
    outgoing,
    trimmed,
    partial,
    sums,
    local_sem,
    send_sem,
    bundle_recv,
    recv_sem,
    summary_send,
    summary_recv,
    sum_send,
    sum_recv,
    gather_send,
    z_recv,
    x_recv,
    half_recv,
    last_recv,
    four_recv,
    out_sem,
    above_sem,
    ring_sem,
    core_sem,
):
    me = lax.axis_index("rep")
    shard = lax.axis_index("shard")
    z, x = me // NX, lax.rem(me, NX)

    def at(dz, dx):
        return lax.rem(z + dz, NZ) * NX + lax.rem(x + dx, NX)

    y, core = shard // 2, lax.rem(shard, 2)

    def in_y(dy):
        return lax.rem(y + dy, NY) * 2 + core

    local = [
        pltpu.make_async_copy(src, dst, local_sem.at[i])
        for i, (src, dst) in enumerate(
            (
                (half_row(grads, me, 0), received.at[direct(0, x)]),
                (half_row(grads, me, 1), received.at[direct(1, x)]),
                (half_row(grads, at(NZ - 1, 0), 0), received.at[bundle(0, x)]),
                (half_row(grads, at(1, 0), 1), received.at[bundle(1, x)]),
                (row_of(weight, me), row),
                (moment_one, one_ref),
                (moment_two, two_ref),
            )
        )
    ]

    barrier = pltpu.get_barrier_semaphore()

    def signal(sem, rep, sh):
        pl.semaphore_signal(sem, inc=1, device_id=(rep, sh), device_id_type=MESH)

    for dx in (2, 1, 3):
        signal(barrier, at(0, dx), shard)
    for dy in (1, NY - 1):
        signal(barrier, me, in_y(dy))

    @pl.when(core == 0)
    def _():
        signal(barrier, me, shard + 1)

    @pl.loop(z + 1, NZ)
    def _(zz):
        for xx in range(NX):
            signal(barrier, zz * NX + xx, shard)

    pl.semaphore_wait(barrier, 5 + NX * z + core)

    @pl.loop(0, z)
    def _(zz):
        signal(above_sem.at[z], zz * NX + x, shard)

    def send_half(row_index, h, slot, peer, sem):
        pltpu.make_async_remote_copy(
            src_ref=half_row(grads, row_index, h),
            dst_ref=received.at[slot],
            send_sem=send_sem,
            recv_sem=sem,
            device_id=(peer, shard),
            device_id_type=MESH,
        ).start()

    def towards(zz):
        d = lax.rem(zz - z + NZ, NZ)
        down = (d > NZ // 2).astype(jnp.int32)
        distance = d + down * (NZ - 2 * d)
        return down, distance, d != NZ // 2

    def send_bundles(zz):
        down, distance, far = towards(zz)
        beyond = lax.rem(zz + 1 + down * (NZ - 2), NZ)

        @pl.when(far)
        def _():
            for dx in (2, 1, 3, 0):
                xx = lax.rem(x + dx, NX)
                slot = bundle(1 - down, distance * NX + x)
                send_half(beyond * NX + xx, 1 - down, slot, zz * NX + xx, bundle_recv.at[1 - down])

    def send_direct(zz):
        down, distance, far = towards(zz)

        @pl.when(far)
        def _():
            for dx in (2, 1, 3, 0):
                xx = lax.rem(x + dx, NX)
                slot = direct(down, distance * NX + x)
                send_half(zz * NX + xx, down, slot, zz * NX + xx, recv_sem)

    pl.loop(0, z)(send_bundles)

    for dx in (2, 1, 3):
        send_half(at(NZ - 1, dx), 0, bundle(0, x), at(0, dx), bundle_recv.at[0])
        send_half(at(1, dx), 1, bundle(1, x), at(0, dx), bundle_recv.at[1])

    pl.loop(0, z)(send_direct)

    for dx in (2, 1, 3):
        for h in range(2):
            send_half(at(0, dx), h, direct(h, x), at(0, dx), recv_sem)

    @pl.loop(z + 1, NZ)
    def _(zz):
        pl.semaphore_wait(above_sem.at[zz], 1)
        send_bundles(zz)

        @pl.when(zz - 1 > z)
        def _():
            send_direct(zz - 1)

    pl.loop(jnp.maximum(z + 1, NZ - 1), NZ)(send_direct)

    for copy in local:
        copy.start()

    @pl.when(core == 0)
    def _():
        pl.semaphore_wait(core_sem, 1)

    signal(core_sem, me, shard + 1 - 2 * core)

    @pl.when(core == 1)
    def _():
        pl.semaphore_wait(core_sem, 1)

    for r in range(NY // 2 - 1):
        for side, dy in enumerate((1, NY - 1)):
            signal(ring_sem.at[r, side], me, in_y(dy))
        for side in range(2):
            pl.semaphore_wait(ring_sem.at[r, side], 1)

    for copy in local:
        copy.wait()
    def came(view, sem):
        pltpu.make_async_copy(view, view, sem).wait()

    def halves(n):
        return received.at[pl.ds(0, n)]

    def condense(first_slot):
        @pl.loop(0, 5)
        def _(j):
            rows = pl.ds(pl.multiple_of(j * 8, 8), 8)
            values = [received[first_slot + i, rows, :] for i in range(16)]
            (low, high), rest = merge(sort8(values[:8]), sort8(values[8:]))
            for i, value in enumerate(low + high + [rest]):
                received[first_slot + i, rows, :] = value

    for h, dz in enumerate((NZ - 1, 1)):
        came(halves(15), bundle_recv.at[h])
        condense(bundle(h, 0))
        pltpu.make_async_remote_copy(
            src_ref=received.at[pl.ds(bundle(h, 0), 9)],
            dst_ref=summary.at[h],
            send_sem=summary_send,
            recv_sem=summary_recv.at[h],
            device_id=(at(dz, 0), shard),
            device_id_type=MESH,
        ).start()
    came(halves(30), recv_sem)
    for h in range(2):
        condense(direct(h, 0))
    for h in range(2):
        came(halves(9), summary_recv.at[h])

    def block(j, squares):
        h, rows = j // 5, pl.ds(pl.multiple_of(lax.rem(j, 5) * 8, 8), 8)
        near = [received[direct(h, i), rows, :] for i in range(9)]
        far = [summary[h, i, rows, :] for i in range(9)]
        rest = middle((near[:4], near[4:8]), (far[:4], far[4:8]))
        mean = (near[8] + far[8] + rest) / (REPS - 2 * TRIM)
        trimmed[h, rows, :] = mean
        return squares + mean * mean

    squares = lax.fori_loop(0, 10, block, jnp.zeros((8, 128), F32))
    total = jnp.sum(squares, axis=0, keepdims=True)

    stages = (
        (2 * REPS, me * 2 + core, lambda p: (p // 2, y * 2 + lax.rem(p, 2))),
        (NY, y, lambda p: (me, p * 2 + core)),
    )
    for stage, (count, mine, device) in enumerate(stages):
        partial[stage] = total
        sums[stage, pl.ds(mine, 1), :] = total
        for i in range(1, count):
            pltpu.make_async_remote_copy(
                src_ref=partial.at[stage],
                dst_ref=sums.at[stage, pl.ds(mine, 1), :],
                send_sem=sum_send.at[stage],
                recv_sem=sum_recv.at[stage],
                device_id=device(lax.rem(mine + i, count)),
                device_id_type=MESH,
            ).start()
        got = sums.at[stage, pl.ds(0, count - 1), :]
        pltpu.make_async_copy(got, got, sum_recv.at[stage]).wait()
        total = jnp.sum(sums[stage, 0:count, :], axis=0, keepdims=True)
    total = jnp.sum(total, axis=1, keepdims=True)
    factor = jnp.minimum(1.0, 1.0 / jnp.sqrt(total / params + 1e-12))

    clipped = factor * trimmed[...]
    new_one = 0.9 * one_ref[...] + 0.1 * clipped
    new_two = 0.95 * two_ref[...] + 0.05 * clipped * clipped
    update = new_one / (1.0 - 0.9**STEP) / (jnp.sqrt(new_two / (1.0 - 0.95**STEP)) + 1e-08)
    owned = row[...]
    outgoing[...] = owned - 0.05 * (update + 0.1 * owned)
    new_one_ref[...] = new_one
    new_two_ref[...] = new_two

    first, last = pl.ds(0, SPLIT), pl.ds(SPLIT, 40 - SPLIT)
    right_left = (1, NX - 1)

    def part(r, tiles):
        return new_weight.at[:, r // 8, tiles, lax.rem(r, 8), :]

    def half(r, h):
        return new_weight.at[h, r // 8, first, lax.rem(r, 8), :]

    def four(zz):
        return new_weight.at[:, zz // 2, last, pl.ds(lax.rem(zz, 2) * 4, 4), :]

    def half_four(zz, h):
        return new_weight.at[h, zz // 2, last, pl.ds(lax.rem(zz, 2) * 4, 4), :]

    def push(src, dst, peer, sem):
        pltpu.make_async_remote_copy(
            src_ref=src,
            dst_ref=dst,
            send_sem=gather_send,
            recv_sem=sem,
            device_id=(peer, shard),
            device_id_type=MESH,
        ).start()

    def zs(dz):
        return lax.rem(z + dz, NZ)

    def along_x(dz, src=None):
        view = part(at(dz, 0), first)
        for side, dx in enumerate(right_left):
            push(view if src is None else src, view, at(0, dx), x_recv.at[side, zs(dz)])

    def relay_x(dz):
        for side, dx in enumerate(right_left):
            r = at(dz, NX - dx)
            came(part(r, first), x_recv.at[side, zs(dz)])
            push(half(r, side), half(r, side), at(0, dx), half_recv)

    def across_x(dz):
        view = part(at(dz, 0), first)
        push(view, view, at(0, 2), half_recv)

    def arrive_x(dz):
        for side, dx in enumerate(right_left):
            came(part(at(dz, NX - dx), first), x_recv.at[side, zs(dz)])

    def from_z(dz):
        came(part(at(dz, 0), first), z_recv.at[zs(dz)])

    own_first, own_last = outgoing.at[:, first, :], outgoing.at[:, last, :]
    for dz in (2, 6, 1, 7):
        push(own_first, part(me, first), at(dz, 0), z_recv.at[z])
    along_x(0, own_first)
    for dx in (2, 1, 3):
        push(own_last, part(me, last), at(0, dx), last_recv)
    keep = pltpu.make_async_copy(outgoing, row_of(new_weight, me), out_sem)
    keep.start()

    for dz in (1, 7):
        from_z(dz)
        along_x(dz)
    for dz, on in ((6, 1), (2, 7)):
        from_z(dz)
        r, h = at(dz, 0), (0 if on == 1 else 1)
        push(part(r, first), part(r, first), at(on, 0), z_recv.at[zs(dz)])
        push(half(r, h), half(r, h), at(2 * on % NZ, 0), z_recv.at[zs(dz)])
        along_x(dz)
    relay_x(0)
    three = received.at[pl.ds(0, 6), last, :]
    came(three, last_recv)
    keep.wait()
    for dz in (2, 6, 1, 7):
        push(four(z), four(z), at(dz, 0), four_recv.at[z])
    for dz in (3, 5, 4):
        from_z(dz)
        if dz == 4:
            across_x(dz)
        along_x(dz)
    for dz in (1, 7, 2, 6):
        relay_x(dz)
    for dz, on in ((6, 1), (2, 7)):
        zz, h = zs(dz), (0 if on == 1 else 1)
        came(four(zz), four_recv.at[zz])
        push(four(zz), four(zz), at(on, 0), four_recv.at[zz])
        push(half_four(zz, h), half_four(zz, h), at(2 * on % NZ, 0), four_recv.at[zz])
    for dz in (3, 5):
        relay_x(dz)
    arrive_x(4)
    for dz in (1, 7, 3, 5, 4):
        came(four(zs(dz)), four_recv.at[zs(dz)])
    came(received.at[pl.ds(0, 16), first, :], half_recv)

    came(halves(60), send_sem)
    came(halves(18), summary_send)
    came(halves(62), gather_send)
    for stage, (count, _, _) in enumerate(stages):
        got = sums.at[stage, pl.ds(0, count - 1), :]
        pltpu.make_async_copy(got, got, sum_send.at[stage]).wait()


def store(*refs):
    *pairs, sems = refs
    copies = [pltpu.make_async_copy(pairs[i], pairs[i + 3], sems.at[i]) for i in range(3)]
    for copy in copies:
        copy.start()
    for copy in copies:
        copy.wait()


def pinned(array):
    return pltpu.with_memory_space_constraint(array, pltpu.HBM)


def on_device(grads, weight, moment_one, moment_two):
    params = weight.shape[0] * SHARDS * weight.shape[1] * weight.shape[2]
    vmem = pl.BlockSpec(memory_space=pltpu.VMEM)
    hbm = pl.BlockSpec(memory_space=pltpu.HBM)
    unit = (2, 40, 128)
    dma, regular = pltpu.SemaphoreType.DMA, pltpu.SemaphoreType.REGULAR
    results = pl.pallas_call(
        lambda *refs: kernel(params, *refs),
        name="robust_step",
        out_shape=(
            pltpu.VMEM((2, 4, 40, 8, 128), F32),
            pltpu.VMEM(unit, F32),
            pltpu.VMEM(unit, F32),
        ),
        in_specs=[hbm] * 4,
        out_specs=(vmem, vmem, vmem),
        scratch_shapes=[
            pltpu.VMEM((2 * REPS, 40, 128), F32),
            pltpu.VMEM((2, 9, 40, 128), F32),
            pltpu.VMEM(unit, F32),
            pltpu.VMEM(unit, F32),
            pltpu.VMEM(unit, F32),
            pltpu.VMEM(unit, F32),
            pltpu.VMEM(unit, F32),
            pltpu.VMEM((2, 1, 128), F32),
            pltpu.VMEM((2, 2 * REPS, 128), F32),
            dma((7,)),
            dma,
            dma((2,)),
            dma,
            dma,
            dma((2,)),
            dma((2,)),
            dma((2,)),
            dma,
            dma((NZ,)),
            dma((2, NZ)),
            dma,
            dma,
            dma((NZ,)),
            dma,
            regular((NZ,)),
            regular((NY // 2 - 1, 2)),
            regular,
        ],
        compiler_params=pltpu.CompilerParams(
            collective_id=0, has_side_effects=True, vmem_limit_bytes=32 << 20
        ),
    )(pinned(tiles(grads[0])), pinned(tiles(weight)), pinned(moment_one.reshape(unit)), pinned(moment_two.reshape(unit)))
    new_weight, new_one, new_two = pl.pallas_call(
        store,
        name="store",
        out_shape=tuple(jax.ShapeDtypeStruct(r.shape, F32) for r in results),
        in_specs=[vmem] * 3,
        out_specs=(hbm,) * 3,
        scratch_shapes=[dma((3,))],
        compiler_params=pltpu.CompilerParams(vmem_limit_bytes=16 << 20),
    )(*results)
    return (
        new_weight.transpose(0, 1, 3, 2, 4).reshape(weight.shape),
        new_one.reshape(moment_one.shape),
        new_two.reshape(moment_two.shape),
    )


def solution(mesh):
    return jax.shard_map(
        on_device,
        mesh=mesh,
        in_specs=(
            P("rep", "shard", None, None),
            P("shard", None, None),
            P("shard", "rep", None),
            P("shard", "rep", None),
        ),
        out_specs=(P("shard", None, None), P("shard", "rep", None), P("shard", "rep", None)),
        check_vma=False,
    )
```
